512 devices in a mesh: gx: 8 (over z), gy: 8 (over y_lo, core), gz: 8 (over y_hi, x).
Axes of the slice: x: 4, y: 8 (y_hi: 2, y_lo: 4; y = y_hi * 4 + y_lo), z: 8, core: 2. Of those that a mesh axis runs over, the one named last changes fastest.
Arguments:
- x_in: bfloat16 [3072, 5120], P(('gy', 'gx'), 'gz'), may hold values from -190 to 190
- gain: float32 [5120], P('gz'), may hold values from 0.25 to 1.75
- w_up: bfloat16 [5120, 7168], P(('gz', 'gy'), 'gx'), may hold values from -0.078125 to 0.078125
- w_down: bfloat16 [7168, 5120], P(('gx', 'gy'), 'gz'), may hold values from -0.0625 to 0.0625
- d_out: bfloat16 [3072, 5120], P(('gy', 'gx'), 'gz'), may hold values from -1.1953125 to 1.1953125
Outputs:
- d_x: bfloat16 [3072, 5120], P(('gy', 'gx'), 'gz')
- d_w_up: bfloat16 [5120, 7168], P(('gz', 'gy'), 'gx')
- d_w_down: bfloat16 [7168, 5120], P(('gx', 'gy'), 'gz')
- d_gain: float32 [5120], P('gz')
The draws below stay inside these ranges and needn't reach their ends.
All inputs are finite; a program needn't handle non-finite values.
Results may differ from the reference program's by a relative error of at most 0.02.
Values may be sent and summed in bfloat16 or wider, within the bound.
No kernel may reach another device: no remote copies, remote signals or barrier semaphores. Data moves between devices by JAX's collectives and lax.ppermute only.
A program may use at most 64 MiB of HBM per device.

```python
import jax
import jax.numpy as jnp
from jax import lax

D = 5120
FF = 7168
TOKENS = 3072
N_GX = 8
N_GY = 8
N_GZ = 8


def draw_x_in(key, part):
    keys = jax.random.split(jax.random.fold_in(key, 11), 4)
    position = jnp.arange(D, dtype=jnp.float32) / D
    column_scale = jnp.exp(1.0986 * position) * jax.random.uniform(keys[0], (D,), jnp.float32, 0.7, 1.4)
    row_scale = jnp.exp(jax.random.uniform(keys[1], (TOKENS, 1), jnp.float32, 0.0, 2.3026))
    offset = 0.5 * jnp.clip(jax.random.normal(keys[2], (TOKENS, 1), jnp.float32), -3.0, 3.0)
    base = jnp.clip(jax.random.normal(keys[3], (TOKENS, D), jnp.float32), -4.0, 4.0)
    return ((base * column_scale + offset) * row_scale).astype(jnp.bfloat16)


def shard_levels(stream_key, dims, shards, least, largest):
    def one(dim, blocks):
        draws = jax.random.uniform(jax.random.fold_in(jax.random.fold_in(stream_key, 6), dim), (blocks,), jnp.float32, least / len(shards), largest / len(shards))
        return jnp.repeat(jnp.exp(draws), dims[dim] // blocks).reshape((-1,) + (1,) * (len(dims) - dim - 1))

    level = one(*shards[0])
    for cut in shards[1:]:
        level = level * one(*cut)
    return level


def gaussian(key, extent, spread, most, shards=(), held_as=jnp.bfloat16):
    loudness = shard_levels(key, extent, shards, -0.22, 0.18) if shards else 1.0
    entries = jax.random.normal(key, extent, jnp.float32) * spread * loudness
    return jnp.minimum(jnp.maximum(entries, -most), most).astype(held_as)


def setup_inputs(seed: int = 0) -> dict:
    splits = jax.random.split(jax.random.key(seed), 6)
    return {
        "x_in": draw_x_in(jax.random.fold_in(splits[5], 71), 0),
        "gain": jnp.clip(1.0 + 0.15 * jax.random.normal(splits[1], (D,), jnp.float32), 0.25, 1.75),
        "w_up": gaussian(splits[2], (D, FF), D ** -0.5, 0.078125, ((0, 64), (1, 8))),
        "w_down": gaussian(splits[3], (FF, D), FF ** -0.5, 0.0625, ((0, 64), (1, 8))),
        "d_out": gaussian(splits[4], (TOKENS, D), 0.2, 1.1953125, ((0, 64), (1, 8))),
    }


def gelu_pair(hidden):
    cdf = 0.5 * (1.0 + jax.scipy.special.erf(hidden * 0.7071067811865476))
    slope = cdf + hidden * jnp.exp(-0.5 * hidden * hidden) * 0.3989422804014327
    return (hidden * cdf, slope)

def rounded(value):
    return lax.optimization_barrier(value.astype(jnp.bfloat16)).astype(jnp.float32)

def reference(x_in, gain, w_up, w_down, d_out):
    xf = x_in.astype(jnp.float32)
    mean = lax.optimization_barrier(jnp.mean(xf, axis=1, keepdims=True))
    centered = xf - mean
    var = lax.optimization_barrier(jnp.mean(centered * centered, axis=1, keepdims=True))
    inv = 1.0 / jnp.sqrt(var + 1e-05)
    normed = centered * inv
    z = (normed * gain).astype(jnp.bfloat16)
    fblock = D // N_GZ
    hidden = jnp.zeros((TOKENS, FF), jnp.float32)
    d_act = jnp.zeros((TOKENS, FF), jnp.float32)
    for index in range(N_GZ):
        lo = index * fblock
        hidden = hidden + rounded(jnp.dot(z[:, lo:lo + fblock], w_up[lo:lo + fblock], preferred_element_type=jnp.float32))
        d_act = d_act + rounded(jnp.dot(d_out[:, lo:lo + fblock], w_down[:, lo:lo + fblock].T, preferred_element_type=jnp.float32))
    act_f, slope = gelu_pair(hidden)
    act = act_f.astype(jnp.bfloat16)
    d_hidden = (d_act * slope).astype(jnp.bfloat16)
    tblock = TOKENS // N_GY
    d_w_down = jnp.zeros((FF, D), jnp.float32)
    d_w_up = jnp.zeros((D, FF), jnp.float32)
    for index in range(N_GY):
        lo = index * tblock
        d_w_down = d_w_down + rounded(jnp.dot(act[lo:lo + tblock].T, d_out[lo:lo + tblock], preferred_element_type=jnp.float32))
        d_w_up = d_w_up + rounded(jnp.dot(z[lo:lo + tblock].T, d_hidden[lo:lo + tblock], preferred_element_type=jnp.float32))
    hblock = FF // N_GX
    d_z = jnp.zeros((TOKENS, D), jnp.float32)
    for index in range(N_GX):
        lo = index * hblock
        d_z = d_z + rounded(jnp.dot(d_hidden[:, lo:lo + hblock], w_up[:, lo:lo + hblock].T, preferred_element_type=jnp.float32))
    d_gain = lax.optimization_barrier(jnp.sum(d_z * normed, axis=0))
    d_scaled = d_z * gain
    first = lax.optimization_barrier(jnp.mean(d_scaled, axis=1, keepdims=True))
    second = lax.optimization_barrier(jnp.mean(d_scaled * normed, axis=1, keepdims=True))
    d_x = (inv * (d_scaled - first - normed * second)).astype(jnp.bfloat16)
    return (d_x, d_w_up.astype(jnp.bfloat16), d_w_down.astype(jnp.bfloat16), d_gain)
```

```python
import jax
import jax.numpy as jnp
from jax import lax
from jax.sharding import PartitionSpec as P

BF, F32 = jnp.bfloat16, jnp.float32


def gelu_pair(hidden):
    cdf = 0.5 * (1.0 + jax.scipy.special.erf(hidden * 0.7071067811865476))
    slope = cdf + hidden * jnp.exp(-0.5 * hidden * hidden) * 0.3989422804014327
    return (hidden * cdf, slope)


def exchange(blocks, axis):
    return lax.all_to_all(blocks, axis, 0, 0, tiled=True)


def spread(value, axis):
    n = lax.axis_size(axis)
    return exchange(jnp.broadcast_to(value[None], (n, *value.shape)), axis)


def summed(blocks):
    return jnp.sum(blocks.astype(F32), axis=0)


def body(x_in, gain, w_up, w_down, d_out):
    rows, local = x_in.shape
    n_gx, n_gy, n_gz = (lax.axis_size(a) for a in ("gx", "gy", "gz"))
    width = local * n_gz
    hid = w_up.shape[1]
    all_rows = rows * n_gx
    block = all_rows // n_gz

    down_full = lax.all_gather(w_down, "gy", axis=0, tiled=True)
    up_full = spread(w_up, "gy").reshape(-1, hid)
    both = lax.all_gather(jnp.concatenate([x_in, d_out], axis=1), "gx", axis=0, tiled=True)
    both, up_full = lax.optimization_barrier((both, up_full))
    x_rows, out_rows = both[:, :local].astype(F32), both[:, local:]

    part_sum = jnp.sum(x_rows, axis=1)
    off = x_rows - (part_sum / local)[:, None]
    stats = spread(jnp.stack([part_sum, jnp.sum(off * off, axis=1)]), "gz")
    sums, seconds = stats[:, 0], stats[:, 1]
    mean = jnp.sum(sums, axis=0) / width
    shift = sums / local - mean
    var = (jnp.sum(seconds, axis=0) + local * jnp.sum(shift * shift, axis=0)) / width
    inv = lax.rsqrt(var + 1e-05)
    normed = (x_rows - mean[:, None]) * inv[:, None]
    z = (normed * gain).astype(BF)

    hid_part = jnp.dot(z, up_full, preferred_element_type=F32).astype(BF)
    dact_part = lax.dot_general(
        out_rows, down_full, (((1,), (1,)), ((), ())), preferred_element_type=F32
    ).astype(BF)
    pair = jnp.concatenate([hid_part, dact_part], axis=1).reshape(n_gz, block, 2 * hid)
    pair = summed(exchange(pair, "gz"))
    hidden, d_act = pair[:, :hid], pair[:, hid:]
    act_f, slope = gelu_pair(hidden)
    d_hidden = (d_act * slope).astype(BF)
    cross = jnp.sum(d_hidden.astype(F32) * hidden, axis=1)
    tilt = jnp.sum(up_full.astype(F32) * gain[:, None], axis=0)
    small = lax.all_gather(jnp.concatenate([tilt, cross]), "gz")
    acts = spread(jnp.concatenate([act_f.astype(BF), d_hidden], axis=1), "gz")
    acts, small = lax.optimization_barrier((acts, small))
    acts = acts.reshape(all_rows, 2 * hid)
    act_rows, hgrad_rows = acts[:, :hid], acts[:, hid:]
    tilt = jnp.sum(small[:, :hid], axis=0)
    cross = small[:, hid:].reshape(all_rows)

    dz_part = lax.dot_general(
        hgrad_rows, up_full, (((1,), (1,)), ((), ())), preferred_element_type=F32
    )
    level = jnp.sum(hgrad_rows.astype(F32) * tilt, axis=1)
    gain_part = jnp.sum(dz_part * normed, axis=0)
    tail = lax.psum(jnp.concatenate([level, cross, gain_part]), "gx")
    d_w_up = lax.dot_general(
        z, hgrad_rows, (((0,), (0,)), ((), ())), preferred_element_type=F32
    ).astype(BF)
    d_w_up, tail = lax.optimization_barrier((d_w_up, tail))
    d_gain = jnp.sum(lax.all_gather(tail[2 * all_rows :], "gy"), axis=0)

    d_z = summed(exchange(dz_part.astype(BF).reshape(n_gx, rows, local), "gx"))
    d_w_down = lax.psum_scatter(
        lax.dot_general(
            act_rows, out_rows, (((0,), (0,)), ((), ())), preferred_element_type=F32
        ).astype(BF),
        "gy",
        scatter_dimension=0,
        tiled=True,
    )
    d_w_up = summed(exchange(d_w_up.reshape(n_gy, -1, hid), "gy")).astype(BF)

    first = lax.axis_index("gx") * rows

    def own(values):
        return lax.dynamic_slice(values, (first,), (rows,))[:, None]

    own_inv = own(inv)
    own_normed = (x_in.astype(F32) - own(mean)) * own_inv
    scaled_sum, cross_sum = own(tail[:all_rows]), own(tail[all_rows : 2 * all_rows])
    d_x = own_inv * (d_z * gain - scaled_sum / width - own_normed * (cross_sum / width))
    return (d_x.astype(BF), d_w_up, d_w_down, d_gain)


def solution(mesh):
    placed = (
        P(("gy", "gx"), "gz"),
        P("gz"),
        P(("gz", "gy"), "gx"),
        P(("gx", "gy"), "gz"),
        P(("gy", "gx"), "gz"),
    )
    return jax.shard_map(
        body,
        mesh=mesh,
        in_specs=placed,
        out_specs=(P(("gy", "gx"), "gz"), P(("gz", "gy"), "gx"), P(("gx", "gy"), "gz"), P("gz")),
        check_vma=False,
    )
```

```python
import jax
import jax.numpy as jnp
from jax import lax
from jax.sharding import Mesh
from jax.sharding import PartitionSpec as P

BF, F32 = jnp.bfloat16, jnp.float32
LANES = 128
GY, GZ = ("yl", "co"), ("yh", "xx")


def gelu_pair(hidden):
    cdf = 0.5 * (1.0 + jax.scipy.special.erf(hidden * 0.7071067811865476))
    slope = cdf + hidden * jnp.exp(-0.5 * hidden * hidden) * 0.3989422804014327
    return (hidden * cdf, slope)


def exchange(blocks, axis):
    return lax.all_to_all(blocks, axis, 0, 0, tiled=True)


def spread(value, axis):
    n = lax.axis_size(axis)
    return exchange(jnp.broadcast_to(value[None], (n, *value.shape)), axis)


def summed(blocks):
    return jnp.sum(blocks.astype(F32), axis=0)


def pieces(value):
    high = lax.reduce_precision(value, 8, 7)
    rest = value - high
    middle = lax.reduce_precision(rest, 8, 7)
    return [p.astype(BF) for p in (high, middle, rest - middle)]


def columns(values, rows):
    cols = jnp.stack([p for v in values for p in pieces(v)], axis=1)
    return jnp.pad(cols, ((0, 0), (0, LANES - cols.shape[1])))


def other_core(value):
    return lax.ppermute(value, "co", [(0, 1), (1, 0)])


def body(x_in, gain, w_up, w_down, d_out):
    rows, local = x_in.shape
    n_gx, n_yl, n_gz = (lax.axis_size(a) for a in ("gx", "yl", GZ))
    width = local * n_gz
    hid = w_up.shape[1]
    all_rows = rows * n_gx
    block = all_rows // n_gz
    core = lax.axis_index("co")

    down_full = lax.all_gather(w_down, GY, axis=0, tiled=True)
    up_mine = spread(w_up, "yl")
    both = lax.all_gather(jnp.concatenate([x_in, d_out], axis=1), "gx", axis=0, tiled=True)
    both, up_mine = lax.optimization_barrier((both, up_mine))
    up_other = other_core(up_mine)
    even = core == 0
    up_full = jnp.stack(
        [jnp.where(even, up_mine, up_other), jnp.where(even, up_other, up_mine)], axis=1
    ).reshape(local, hid)
    x_rows, out_rows = both[:, :local].astype(F32), both[:, local:]

    part_sum = jnp.sum(x_rows, axis=1)
    off = x_rows - (part_sum / local)[:, None]
    own_gain = gain.reshape(n_yl, 2, -1, 1)
    own_gain = jnp.where(even, own_gain[:, 0], own_gain[:, 1])
    tilt = jnp.sum(up_mine.astype(F32) * own_gain, axis=(0, 1))
    stats = spread(jnp.concatenate([part_sum, jnp.sum(off * off, axis=1), tilt])[None], GZ)[:, 0]
    sums, seconds = stats[:, :all_rows], stats[:, all_rows : 2 * all_rows]
    tilt = jnp.sum(stats[:, 2 * all_rows :], axis=0)
    tilt = tilt + other_core(tilt)
    mean = jnp.sum(sums, axis=0) / width
    shift = sums / local - mean
    var = (jnp.sum(seconds, axis=0) + local * jnp.sum(shift * shift, axis=0)) / width
    inv = lax.rsqrt(var + 1e-05)
    normed = (x_rows - mean[:, None]) * inv[:, None]
    z = (normed * gain).astype(BF)

    hid_part = jnp.dot(z, up_full, preferred_element_type=F32).astype(BF)
    dact_part = lax.dot_general(
        out_rows, down_full, (((1,), (1,)), ((), ())), preferred_element_type=F32
    ).astype(BF)
    pair = jnp.concatenate([hid_part, dact_part], axis=1).reshape(n_gz, block, 2 * hid)
    pair = summed(exchange(pair, GZ))
    hidden, d_act = pair[:, :hid], pair[:, hid:]
    act_f, slope = gelu_pair(hidden)
    d_hidden = (d_act * slope).astype(BF)
    cross = jnp.sum(d_hidden.astype(F32) * hidden, axis=1)
    acts = jnp.concatenate([act_f.astype(BF), d_hidden, columns([cross], block)], axis=1)
    acts = spread(acts, GZ).reshape(all_rows, -1)
    act_rows, hgrad_rows = acts[:, :hid], acts[:, hid : 2 * hid]
    cross = jnp.sum(acts[:, 2 * hid : 2 * hid + 3].astype(F32), axis=1)

    down_part = lax.dot_general(
        act_rows, out_rows, (((0,), (0,)), ((), ())), preferred_element_type=F32
    ).astype(BF)
    down_part, hgrad_rows = lax.optimization_barrier((down_part, hgrad_rows))
    d_w_down = lax.psum_scatter(down_part, GY, scatter_dimension=0, tiled=True)

    dz_part = lax.dot_general(
        hgrad_rows, up_full, (((1,), (1,)), ((), ())), preferred_element_type=F32
    )
    level = jnp.sum(hgrad_rows.astype(F32) * tilt, axis=1)
    gain_part = jnp.concatenate(
        [p.reshape(-1, LANES) for p in pieces(jnp.sum(dz_part * normed, axis=0))]
    )
    gain_rows = gain_part.shape[0]
    gain_part = jnp.pad(gain_part, ((0, rows - gain_rows), (0, 0)))
    tail = jnp.concatenate(
        [
            dz_part.astype(BF).reshape(n_gx, rows, local),
            columns([level, cross], all_rows).reshape(n_gx, rows, LANES),
            jnp.broadcast_to(gain_part, (n_gx, rows, LANES)),
        ],
        axis=2,
    )
    tail = summed(exchange(tail, "gx"))
    d_z = tail[:, :local]
    scaled_sum = jnp.sum(tail[:, local : local + 3], axis=1, keepdims=True)
    cross_sum = jnp.sum(tail[:, local + 3 : local + 6], axis=1, keepdims=True)
    gain_part = jnp.sum(tail[:gain_rows, local + LANES :].reshape(3, local), axis=0)

    d_w_up = lax.dot_general(
        z, hgrad_rows, (((0,), (0,)), ((), ())), preferred_element_type=F32
    ).astype(BF)
    d_w_up = d_w_up.reshape(n_yl, 2, -1, hid)
    keep = jnp.where(even, d_w_up[:, 0], d_w_up[:, 1])
    give = jnp.where(even, d_w_up[:, 1], d_w_up[:, 0])
    d_w_up = (keep.astype(F32) + other_core(give).astype(F32)).astype(BF)
    gain_part = jnp.pad(jnp.stack(pieces(gain_part)), ((0, 5), (0, hid - local)))
    d_w_up = jnp.concatenate(
        [d_w_up, jnp.broadcast_to(gain_part, (n_yl, *gain_part.shape))], axis=1
    )
    d_w_up = summed(exchange(d_w_up, "yl"))
    height = w_up.shape[0]
    d_gain = jnp.sum(d_w_up[height : height + 3, :local], axis=0)
    d_w_up = d_w_up[:height].astype(BF)
    d_gain = d_gain + other_core(d_gain)

    first = lax.axis_index("gx") * rows

    def own(values):
        return lax.dynamic_slice(values, (first,), (rows,))[:, None]

    d_z, d_w_down = lax.optimization_barrier((d_z, d_w_down))
    own_inv = own(inv)
    own_normed = (x_in.astype(F32) - own(mean)) * own_inv
    d_x = own_inv * (d_z * gain - scaled_sum / width - own_normed * (cross_sum / width))
    return (d_x.astype(BF), d_w_up, d_w_down, d_gain)


def solution(mesh):
    sizes = mesh.shape
    cores, x_chips = 2, sizes["gz"] // 2
    fine = Mesh(
        mesh.devices.reshape(sizes["gx"], sizes["gy"] // cores, cores, 2, x_chips),
        ("gx", *GY, *GZ),
    )
    placed = (
        P((*GY, "gx"), GZ),
        P(GZ),
        P((*GZ, *GY), "gx"),
        P(("gx", *GY), GZ),
        P((*GY, "gx"), GZ),
    )
    return jax.shard_map(
        body,
        mesh=fine,
        in_specs=placed,
        out_specs=(P((*GY, "gx"), GZ), P((*GZ, *GY), "gx"), P(("gx", *GY), GZ), P(GZ)),
        check_vma=False,
    )
```

```python
import jax
import jax.numpy as jnp
from jax import lax
from jax.sharding import Mesh
from jax.sharding import PartitionSpec as P

BF, F32 = jnp.bfloat16, jnp.float32
LANES = 128
GY, GZ = ("yl", "co"), ("yh", "xx")


def gelu_pair(hidden):
    cdf = 0.5 * (1.0 + jax.scipy.special.erf(hidden * 0.7071067811865476))
    slope = cdf + hidden * jnp.exp(-0.5 * hidden * hidden) * 0.3989422804014327
    return (hidden * cdf, slope)


def exchange(blocks, axis):
    return lax.all_to_all(blocks, axis, 0, 0, tiled=True)


def spread(value, axis):
    n = lax.axis_size(axis)
    return exchange(jnp.broadcast_to(value[None], (n, *value.shape)), axis)


def summed(blocks):
    return jnp.sum(blocks.astype(F32), axis=0)


def pieces(value):
    high = lax.reduce_precision(value, 8, 7)
    rest = value - high
    middle = lax.reduce_precision(rest, 8, 7)
    return [p.astype(BF) for p in (high, middle, rest - middle)]


def columns(*values):
    return jnp.stack([p for v in values for p in pieces(v)], axis=-1)


def column(lanes, index):
    return jnp.sum(lanes[..., 3 * index : 3 * index + 3].astype(F32), axis=-1)


def other_core(value):
    return lax.ppermute(value, "co", [(0, 1), (1, 0)])


def dot(a, b, contract):
    return lax.dot_general(a, b, ((contract[:1], contract[1:]), ((), ())), preferred_element_type=F32)


def body(x_in, gain, w_up, w_down, d_out):
    rows, local = x_in.shape
    n_gx, n_yl, n_gz = (lax.axis_size(a) for a in ("gx", "yl", GZ))
    width = local * n_gz
    up_rows, hid = w_up.shape
    down_rows = w_down.shape[0]
    all_rows = rows * n_gx
    block = all_rows // n_gz
    even = lax.axis_index("co") == 0

    def by_core(mine, other):
        pair = [jnp.where(even, mine, other), jnp.where(even, other, mine)]
        return jnp.stack(pair, axis=1).reshape(-1, mine.shape[-1])

    down_full = lax.all_gather(w_down, GY, axis=0, tiled=True)
    up_mine = spread(w_up, "yl")
    both = lax.all_gather(jnp.concatenate([x_in, d_out], axis=1), "gx", axis=0, tiled=True)
    both, up_mine = lax.optimization_barrier((both, up_mine))
    up_full = by_core(up_mine, other_core(up_mine))
    x_rows, out_rows = both[:, :local].astype(F32), both[:, local:]

    part_sum = jnp.sum(x_rows, axis=1)
    off = x_rows - (part_sum / local)[:, None]
    second = jnp.sum(off * off, axis=1)
    y = (off * gain).astype(BF)
    gains = jnp.pad(jnp.stack(pieces(gain)), ((0, 5), (0, 0)))
    tilt = jnp.sum(dot(gains, up_full, (1, 0)), axis=0)
    tilt = jnp.stack(pieces(tilt)).reshape(3 * n_gz, -1)
    spare = LANES - tilt.shape[1]
    tilt = jnp.pad(tilt, ((0, block - tilt.shape[0]), (0, 0)))
    marks = columns(part_sum, second)
    extra = jnp.concatenate(
        [
            jnp.pad(marks, ((0, 0), (0, spare - marks.shape[1]))).reshape(n_gz, block, spare),
            jnp.broadcast_to(tilt, (n_gz, *tilt.shape)),
        ],
        axis=2,
    )
    pair = jnp.concatenate(
        [
            dot(y, up_full, (1, 0)).astype(BF).reshape(n_gz, block, hid),
            dot(out_rows, down_full, (1, 1)).astype(BF).reshape(n_gz, block, hid),
            extra,
        ],
        axis=2,
    )
    pair = exchange(pair, GZ)
    marks = pair[:, :, 2 * hid : 2 * hid + spare]
    tilts = pair[:, : 3 * n_gz, 2 * hid + spare :].astype(F32)
    tilts = jnp.sum(tilts.reshape(n_gz, 3, n_gz, -1), axis=1).reshape(n_gz, hid)
    means = column(marks, 0) / local
    mean = jnp.sum(means, axis=0) / n_gz
    shift = means - mean
    var = (jnp.sum(column(marks, 1), axis=0) + local * jnp.sum(shift * shift, axis=0)) / width
    inv = lax.rsqrt(var + 1e-05)
    hidden = summed(pair[:, :, :hid]) + sum(
        shift[i][:, None] * tilts[i][None] for i in range(n_gz)
    )
    hidden = hidden * inv[:, None]
    d_act = summed(pair[:, :, hid : 2 * hid])
    act_f, slope = gelu_pair(hidden)
    d_hidden = (d_act * slope).astype(BF)
    cross = jnp.sum(d_hidden.astype(F32) * hidden, axis=1)
    marks = columns(cross, mean, inv)
    marks = jnp.pad(marks, ((0, 0), (0, LANES - marks.shape[1])))
    acts = jnp.concatenate([act_f.astype(BF), d_hidden, marks], axis=1)
    acts = spread(acts, GZ).reshape(all_rows, -1)
    act_rows, hgrad_rows, marks = acts[:, :hid], acts[:, hid : 2 * hid], acts[:, 2 * hid :]
    cross, mean, inv = (column(marks, i) for i in range(3))
    normed = (x_rows - mean[:, None]) * inv[:, None]
    z = (normed * gain).astype(BF)

    dz_part = dot(hgrad_rows, up_full, (1, 1))
    d_z = lax.psum_scatter(dz_part.astype(BF), "gx", scatter_dimension=0, tiled=True)
    level = jnp.sum(hgrad_rows.astype(F32) * jnp.sum(tilts, axis=0), axis=1)
    gain_part = jnp.sum(dz_part * normed, axis=0)
    tail = jnp.concatenate(
        [
            jnp.broadcast_to(gain_part, (n_gx, local)),
            level.reshape(n_gx, rows),
            cross.reshape(n_gx, rows),
        ],
        axis=1,
    )
    tail = jnp.sum(exchange(tail[:, None], "gx")[:, 0], axis=0)
    scaled_sum = tail[local : local + rows, None] / width
    cross_sum = tail[local + rows :, None] / width

    grads = jnp.concatenate(
        [
            dot(act_rows, out_rows, (0, 0)).astype(BF).reshape(n_yl, 2, down_rows, local),
            jnp.pad(
                dot(z, hgrad_rows, (0, 0)).astype(BF).reshape(n_yl, 2, up_rows, hid),
                ((0, 0), (0, 0), (0, down_rows - up_rows), (0, 0)),
            ),
        ],
        axis=3,
    )
    keep = jnp.where(even, grads[:, 0], grads[:, 1])
    give = jnp.where(even, grads[:, 1], grads[:, 0])
    gain_part = jnp.pad(
        jnp.stack(pieces(tail[:local])),
        ((up_rows, down_rows - up_rows - 3), (local, hid - local)),
    )
    grads = (keep.astype(F32) + other_core(give).astype(F32) + gain_part.astype(F32)).astype(BF)
    grads = summed(exchange(grads, "yl"))
    d_w_down = grads[:, :local].astype(BF)
    d_w_up = grads[:up_rows, local:].astype(BF)
    d_gain = jnp.sum(grads[up_rows : up_rows + 3, local : 2 * local], axis=0)
    d_gain = d_gain + other_core(d_gain)

    first = lax.axis_index("gx") * rows

    def own(values):
        return lax.dynamic_slice(values, (first,), (rows,))[:, None]

    own_inv = own(inv)
    own_normed = (x_in.astype(F32) - own(mean)) * own_inv
    d_x = own_inv * (d_z.astype(F32) * gain - scaled_sum - own_normed * cross_sum)
    return (d_x.astype(BF), d_w_up, d_w_down, d_gain)


def solution(mesh):
    sizes = mesh.shape
    cores, x_chips = 2, sizes["gz"] // 2
    fine = Mesh(
        mesh.devices.reshape(sizes["gx"], sizes["gy"] // cores, cores, 2, x_chips),
        ("gx", *GY, *GZ),
    )
    placed = (
        P((*GY, "gx"), GZ),
        P(GZ),
        P((*GZ, *GY), "gx"),
        P(("gx", *GY), GZ),
        P((*GY, "gx"), GZ),
    )
    return jax.shard_map(
        body,
        mesh=fine,
        in_specs=placed,
        out_specs=(P((*GY, "gx"), GZ), P((*GZ, *GY), "gx"), P(("gx", *GY), GZ), P(GZ)),
        check_vma=False,
    )
```

```python
import jax
import jax.numpy as jnp
from jax import lax
from jax.sharding import Mesh
from jax.sharding import PartitionSpec as P

BF, F32 = jnp.bfloat16, jnp.float32
LANES = 128
GY, GZ = ("yl", "co"), ("yh", "xx")


def gelu_pair(hidden):
    cdf = 0.5 * (1.0 + jax.scipy.special.erf(hidden * 0.7071067811865476))
    slope = cdf + hidden * jnp.exp(-0.5 * hidden * hidden) * 0.3989422804014327
    return (hidden * cdf, slope)


def exchange(blocks, axis):
    return lax.all_to_all(blocks, axis, 0, 0, tiled=True)


def spread(value, axis):
    n = lax.axis_size(axis)
    return exchange(jnp.broadcast_to(value[None], (n, *value.shape)), axis)


def summed(blocks):
    return jnp.sum(blocks.astype(F32), axis=0)


def pieces(value):
    high = lax.reduce_precision(value, 8, 7)
    rest = value - high
    middle = lax.reduce_precision(rest, 8, 7)
    return [p.astype(BF) for p in (high, middle, rest - middle)]


def columns(*values):
    return jnp.stack([p for v in values for p in pieces(v)], axis=-1)


def column(lanes, index):
    return jnp.sum(lanes[..., 3 * index : 3 * index + 3].astype(F32), axis=-1)


def other_core(value):
    return lax.ppermute(value, "co", [(0, 1), (1, 0)])


def dot(a, b, contract):
    return lax.dot_general(a, b, ((contract[:1], contract[1:]), ((), ())), preferred_element_type=F32)


def body(x_in, gain, w_up, w_down, d_out):
    rows, local = x_in.shape
    n_gx, n_yl, n_gz = (lax.axis_size(a) for a in ("gx", "yl", GZ))
    width = local * n_gz
    up_rows, hid = w_up.shape
    down_rows = w_down.shape[0]
    all_rows = rows * n_gx
    block = all_rows // n_gz
    even = lax.axis_index("co") == 0

    def by_core(mine, other):
        pair = [jnp.where(even, mine, other), jnp.where(even, other, mine)]
        return jnp.stack(pair, axis=1).reshape(-1, mine.shape[-1])

    down_full = lax.all_gather(w_down, GY, axis=0, tiled=True)
    up_mine = spread(w_up, "yl")
    both = lax.all_gather(jnp.concatenate([x_in, d_out], axis=1), "gx", axis=0, tiled=True)
    both, up_mine = lax.optimization_barrier((both, up_mine))
    up_full = by_core(up_mine, other_core(up_mine))
    x_rows, out_rows = both[:, :local].astype(F32), both[:, local:]

    part_sum = jnp.sum(x_rows, axis=1)
    off = x_rows - (part_sum / local)[:, None]
    second = jnp.sum(off * off, axis=1)
    y = (off * gain).astype(BF)
    gains = jnp.pad(jnp.stack(pieces(gain)), ((0, 5), (0, 0)))
    tilt = jnp.sum(dot(gains, up_full, (1, 0)), axis=0)
    tilt = jnp.stack(pieces(tilt)).reshape(3 * n_gz, -1)
    spare = LANES - tilt.shape[1]
    tilt = jnp.pad(tilt, ((0, block - tilt.shape[0]), (0, 0)))
    marks = columns(part_sum, second)
    extra = jnp.concatenate(
        [
            jnp.pad(marks, ((0, 0), (0, spare - marks.shape[1]))).reshape(n_gz, block, spare),
            jnp.broadcast_to(tilt, (n_gz, *tilt.shape)),
        ],
        axis=2,
    )
    pair = jnp.concatenate(
        [
            dot(y, up_full, (1, 0)).astype(BF).reshape(n_gz, block, hid),
            dot(out_rows, down_full, (1, 1)).astype(BF).reshape(n_gz, block, hid),
            extra,
        ],
        axis=2,
    )
    pair = exchange(pair, GZ)
    marks = pair[:, :, 2 * hid : 2 * hid + spare]
    tilts = pair[:, : 3 * n_gz, 2 * hid + spare :].astype(F32)
    tilts = jnp.sum(tilts.reshape(n_gz, 3, n_gz, -1), axis=1).reshape(n_gz, hid)
    means = column(marks, 0) / local
    mean = jnp.sum(means, axis=0) / n_gz
    shift = means - mean
    var = (jnp.sum(column(marks, 1), axis=0) + local * jnp.sum(shift * shift, axis=0)) / width
    inv = lax.rsqrt(var + 1e-05)
    hidden = summed(pair[:, :, :hid]) + sum(
        shift[i][:, None] * tilts[i][None] for i in range(n_gz)
    )
    hidden = hidden * inv[:, None]
    d_act = summed(pair[:, :, hid : 2 * hid])
    act_f, slope = gelu_pair(hidden)
    d_hidden = (d_act * slope).astype(BF)
    cross = jnp.sum(d_hidden.astype(F32) * hidden, axis=1)
    marks = columns(cross, mean, inv)
    marks = jnp.pad(marks, ((0, 0), (0, LANES - marks.shape[1])))
    acts = jnp.concatenate([act_f.astype(BF), d_hidden, marks], axis=1)
    acts = spread(acts, GZ).reshape(all_rows, -1)
    act_rows, hgrad_rows, marks = acts[:, :hid], acts[:, hid : 2 * hid], acts[:, 2 * hid :]
    cross, mean, inv = (column(marks, i) for i in range(3))
    normed = (x_rows - mean[:, None]) * inv[:, None]
    z = (normed * gain).astype(BF)

    dz_part = dot(hgrad_rows, up_full, (1, 1))
    level = jnp.sum(hgrad_rows.astype(F32) * jnp.sum(tilts, axis=0), axis=1)
    marks = columns(level, cross)
    tail = jnp.concatenate(
        [dz_part.astype(BF), jnp.pad(marks, ((0, 0), (0, LANES - marks.shape[1])))], axis=1
    ).reshape(n_gx, rows, local + LANES)
    gain_part = jnp.stack(pieces(jnp.sum(dz_part * normed, axis=0)))
    gain_part = jnp.pad(gain_part, ((0, 5), (0, LANES)))
    tail = jnp.concatenate([tail, jnp.broadcast_to(gain_part, (n_gx, *gain_part.shape))], axis=1)
    tail, acts = lax.optimization_barrier((tail, acts))
    act_rows, hgrad_rows = acts[:, :hid], acts[:, hid : 2 * hid]
    tail = exchange(tail, "gx")

    def chunks(value, height):
        cut = [value[:, i : i + LANES] for i in range(0, value.shape[1], LANES)]
        return [c.reshape(n_yl, 2, height, LANES) for c in cut]

    grads = jnp.concatenate(
        [
            *chunks(dot(act_rows, out_rows, (0, 0)).astype(BF), down_rows),
            *chunks(dot(z, hgrad_rows, (0, 0)).astype(BF), up_rows),
        ],
        axis=2,
    )
    keep = jnp.where(even, grads[:, 0], grads[:, 1])
    give = jnp.where(even, grads[:, 1], grads[:, 0])
    swapped, tail = lax.optimization_barrier((other_core(give), tail))
    grads = (keep.astype(F32) + swapped.astype(F32)).astype(BF)
    d_z = summed(tail[:, :rows, :local])
    marks = summed(tail[:, :rows, local:])
    scaled_sum, cross_sum = (column(marks, i)[:, None] / width for i in range(2))
    gain_part = jnp.sum(tail[:, rows : rows + 3, :local].astype(F32), axis=(0, 1))
    gain_part = jnp.concatenate([p.reshape(-1, LANES) for p in pieces(gain_part)])
    gain_rows = gain_part.shape[0]
    gain_part = jnp.pad(gain_part, ((0, -gain_rows % 16), (0, 0)))
    gain_part = jnp.broadcast_to(gain_part, (n_yl, *gain_part.shape))
    start = grads.shape[1]
    grads = jnp.pad(grads, ((0, 0), (0, gain_part.shape[1]), (0, 0)))
    grads = exchange(lax.dynamic_update_slice(grads, gain_part, (0, start, 0)), "yl")

    def unchunk(first, height, count):
        cut = [grads[:, first + i * height : first + (i + 1) * height] for i in range(count)]
        return jnp.concatenate([summed(c).astype(BF) for c in cut], axis=1)

    d_gain = jnp.sum(grads[:, start : start + gain_rows].astype(F32), axis=0)
    d_gain = jnp.sum(d_gain.reshape(3, local), axis=0)
    d_gain = d_gain + other_core(d_gain)
    d_w_down = unchunk(0, down_rows, local // LANES)
    d_w_up = unchunk(down_rows * (local // LANES), up_rows, hid // LANES)

    first = lax.axis_index("gx") * rows

    def own(values):
        return lax.dynamic_slice(values, (first,), (rows,))[:, None]

    own_inv = own(inv)
    own_normed = (x_in.astype(F32) - own(mean)) * own_inv
    d_x = own_inv * (d_z * gain - scaled_sum - own_normed * cross_sum)
    return (d_x.astype(BF), d_w_up, d_w_down, d_gain)


def solution(mesh):
    sizes = mesh.shape
    cores, x_chips = 2, sizes["gz"] // 2
    fine = Mesh(
        mesh.devices.reshape(sizes["gx"], sizes["gy"] // cores, cores, 2, x_chips),
        ("gx", *GY, *GZ),
    )
    placed = (
        P((*GY, "gx"), GZ),
        P(GZ),
        P((*GZ, *GY), "gx"),
        P(("gx", *GY), GZ),
        P((*GY, "gx"), GZ),
    )
    return jax.shard_map(
        body,
        mesh=fine,
        in_specs=placed,
        out_specs=(P((*GY, "gx"), GZ), P((*GZ, *GY), "gx"), P(("gx", *GY), GZ), P(GZ)),
        check_vma=False,
    )
```

```python
import jax
import jax.numpy as jnp
from jax import lax
from jax.sharding import Mesh
from jax.sharding import PartitionSpec as P

BF, F32 = jnp.bfloat16, jnp.float32
LANES = 128
GY, GZ = ("yl", "co"), ("yh", "xx")


def gelu_pair(hidden):
    cdf = 0.5 * (1.0 + jax.scipy.special.erf(hidden * 0.7071067811865476))
    slope = cdf + hidden * jnp.exp(-0.5 * hidden * hidden) * 0.3989422804014327
    return (hidden * cdf, slope)


def exchange(blocks, axis):
    return lax.all_to_all(blocks, axis, 0, 0, tiled=True)


def spread(value, axis):
    n = lax.axis_size(axis)
    return exchange(jnp.broadcast_to(value[None], (n, *value.shape)), axis)


def summed(blocks):
    return jnp.sum(blocks.astype(F32), axis=0)


def pieces(value):
    high = lax.reduce_precision(value, 8, 7)
    rest = value - high
    middle = lax.reduce_precision(rest, 8, 7)
    return [p.astype(BF) for p in (high, middle, rest - middle)]


def columns(*values):
    return jnp.stack([p for v in values for p in pieces(v)], axis=-1)


def column(lanes, index):
    return jnp.sum(lanes[..., 3 * index : 3 * index + 3].astype(F32), axis=-1)


def swap(value, axis, bits):
    return lax.ppermute(value, axis, [(i, i ^ bits) for i in range(lax.axis_size(axis))])


def other_core(value):
    return swap(value, "co", 1)


def dot(a, b, contract):
    return lax.dot_general(a, b, ((contract[:1], contract[1:]), ((), ())), preferred_element_type=F32)


def body(x_in, gain, w_up, w_down, d_out):
    rows, local = x_in.shape
    n_gx, n_yl, n_gz = (lax.axis_size(a) for a in ("gx", "yl", GZ))
    width = local * n_gz
    up_rows, hid = w_up.shape
    down_rows = w_down.shape[0]
    all_rows = rows * n_gx
    block = all_rows // n_gz
    even = lax.axis_index("co") == 0

    def by_core(mine, other):
        pair = [jnp.where(even, mine, other), jnp.where(even, other, mine)]
        return jnp.stack(pair, axis=1).reshape(-1, mine.shape[-1])

    down_full = lax.all_gather(w_down, GY, axis=0, tiled=True)
    up_mine = spread(w_up, "yl")
    both = lax.all_gather(jnp.concatenate([x_in, d_out], axis=1), "gx", axis=0, tiled=True)
    both, up_mine = lax.optimization_barrier((both, up_mine))
    up_full = by_core(up_mine, other_core(up_mine))
    x_rows, out_rows = both[:, :local].astype(F32), both[:, local:]

    part_sum = jnp.sum(x_rows, axis=1)
    off = x_rows - (part_sum / local)[:, None]
    second = jnp.sum(off * off, axis=1)
    y = (off * gain).astype(BF)
    gains = jnp.pad(jnp.stack(pieces(gain)), ((0, 5), (0, 0)))
    tilt = jnp.sum(dot(gains, up_full, (1, 0)), axis=0)
    tilt = jnp.stack(pieces(tilt)).reshape(3 * n_gz, -1)
    spare = LANES - tilt.shape[1]
    tilt = jnp.pad(tilt, ((0, block - tilt.shape[0]), (0, 0)))
    marks = columns(part_sum, second)
    extra = jnp.concatenate(
        [
            jnp.pad(marks, ((0, 0), (0, spare - marks.shape[1]))).reshape(n_gz, block, spare),
            jnp.broadcast_to(tilt, (n_gz, *tilt.shape)),
        ],
        axis=2,
    )
    pair = jnp.concatenate(
        [
            dot(y, up_full, (1, 0)).astype(BF).reshape(n_gz, block, hid),
            dot(out_rows, down_full, (1, 1)).astype(BF).reshape(n_gz, block, hid),
            extra,
        ],
        axis=2,
    )
    pair = exchange(pair, GZ)
    marks = pair[:, :, 2 * hid : 2 * hid + spare]
    tilts = pair[:, : 3 * n_gz, 2 * hid + spare :].astype(F32)
    tilts = jnp.sum(tilts.reshape(n_gz, 3, n_gz, -1), axis=1).reshape(n_gz, hid)
    means = column(marks, 0) / local
    mean = jnp.sum(means, axis=0) / n_gz
    shift = means - mean
    var = (jnp.sum(column(marks, 1), axis=0) + local * jnp.sum(shift * shift, axis=0)) / width
    inv = lax.rsqrt(var + 1e-05)
    hidden = summed(pair[:, :, :hid]) + sum(
        shift[i][:, None] * tilts[i][None] for i in range(n_gz)
    )
    hidden = hidden * inv[:, None]
    d_act = summed(pair[:, :, hid : 2 * hid])
    act_f, slope = gelu_pair(hidden)
    d_hidden = (d_act * slope).astype(BF)
    cross = jnp.sum(d_hidden.astype(F32) * hidden, axis=1)
    marks = columns(cross, mean, inv)
    marks = jnp.pad(marks, ((0, 0), (0, LANES - marks.shape[1])))
    acts = jnp.concatenate([act_f.astype(BF), d_hidden, marks], axis=1)
    acts = spread(acts, GZ).reshape(all_rows, -1)
    act_rows, hgrad_rows, marks = acts[:, :hid], acts[:, hid : 2 * hid], acts[:, 2 * hid :]
    cross, mean, inv = (column(marks, i) for i in range(3))
    normed = (x_rows - mean[:, None]) * inv[:, None]
    z = (normed * gain).astype(BF)

    dz_part = dot(hgrad_rows, up_full, (1, 1))
    level = jnp.sum(hgrad_rows.astype(F32) * jnp.sum(tilts, axis=0), axis=1)
    marks = columns(level, cross)
    tail = jnp.concatenate(
        [dz_part.astype(BF), jnp.pad(marks, ((0, 0), (0, LANES - marks.shape[1])))], axis=1
    ).reshape(n_gx, rows, local + LANES)
    gain_part = jnp.stack(pieces(jnp.sum(dz_part * normed, axis=0)))
    gain_part = jnp.pad(gain_part, ((0, 5), (0, LANES)))
    tail = jnp.concatenate([tail, jnp.broadcast_to(gain_part, (n_gx, *gain_part.shape))], axis=1)
    tail, acts = lax.optimization_barrier((tail, acts))
    act_rows, hgrad_rows = acts[:, :hid], acts[:, hid : 2 * hid]
    tail = exchange(tail, "gx")

    def chunks(value, height):
        cut = [value[:, i : i + LANES] for i in range(0, value.shape[1], LANES)]
        return [c.reshape(n_yl, 2, height, LANES) for c in cut]

    grads = jnp.concatenate(
        [
            *chunks(dot(act_rows, out_rows, (0, 0)).astype(BF), down_rows),
            *chunks(dot(z, hgrad_rows, (0, 0)).astype(BF), up_rows),
        ],
        axis=2,
    )
    keep = jnp.where(even, grads[:, 0], grads[:, 1])
    give = jnp.where(even, grads[:, 1], grads[:, 0])
    grads = (keep.astype(F32) + other_core(give).astype(F32)).astype(BF)
    place = lax.axis_index("yl")

    def part(index):
        return lax.dynamic_index_in_dim(grads, index, keepdims=False)

    grads = [part(place)] + [swap(part(place ^ k), "yl", k) for k in range(1, n_yl)]
    d_z = summed(tail[:, :rows, :local])
    marks = summed(tail[:, :rows, local:])
    scaled_sum, cross_sum = (column(marks, i)[:, None] / width for i in range(2))
    d_gain = jnp.sum(tail[:, rows : rows + 3, :local].astype(F32), axis=(0, 1))
    for axis, bits in (("yl", 1), ("yl", 2), ("co", 1)):
        d_gain = d_gain + swap(d_gain, axis, bits)

    def unchunk(first, height, count):
        cut = [slice(first + i * height, first + (i + 1) * height) for i in range(count)]
        cut = [sum(g[c].astype(F32) for g in grads) for c in cut]
        return jnp.concatenate([c.astype(BF) for c in cut], axis=1)

    d_w_down = unchunk(0, down_rows, local // LANES)
    d_w_up = unchunk(down_rows * (local // LANES), up_rows, hid // LANES)

    first = lax.axis_index("gx") * rows

    def own(values):
        return lax.dynamic_slice(values, (first,), (rows,))[:, None]

    own_inv = own(inv)
    own_normed = (x_in.astype(F32) - own(mean)) * own_inv
    d_x = own_inv * (d_z * gain - scaled_sum - own_normed * cross_sum)
    return (d_x.astype(BF), d_w_up, d_w_down, d_gain)


def solution(mesh):
    sizes = mesh.shape
    cores, x_chips = 2, sizes["gz"] // 2
    fine = Mesh(
        mesh.devices.reshape(sizes["gx"], sizes["gy"] // cores, cores, 2, x_chips),
        ("gx", *GY, *GZ),
    )
    placed = (
        P((*GY, "gx"), GZ),
        P(GZ),
        P((*GZ, *GY), "gx"),
        P(("gx", *GY), GZ),
        P((*GY, "gx"), GZ),
    )
    return jax.shard_map(
        body,
        mesh=fine,
        in_specs=placed,
        out_specs=(P((*GY, "gx"), GZ), P((*GZ, *GY), "gx"), P(("gx", *GY), GZ), P(GZ)),
        check_vma=False,
    )
```

```python
import jax
import jax.numpy as jnp
from jax import lax
from jax.experimental import pallas as pl
from jax.experimental.pallas import tpu as pltpu
from jax.sharding import Mesh
from jax.sharding import PartitionSpec as P

BF, F32 = jnp.bfloat16, jnp.float32
LANES = 128
GY, GZ = ("yl", "co"), ("yh", "xx")


def gelu_pair(hidden):
    cdf = 0.5 * (1.0 + jax.scipy.special.erf(hidden * 0.7071067811865476))
    slope = cdf + hidden * jnp.exp(-0.5 * hidden * hidden) * 0.3989422804014327
    return (hidden * cdf, slope)


def exchange(blocks, axis):
    return lax.all_to_all(blocks, axis, 0, 0, tiled=True)


def spread(value, axis):
    n = lax.axis_size(axis)
    return exchange(jnp.broadcast_to(value[None], (n, *value.shape)), axis)


def summed(blocks):
    return jnp.sum(blocks.astype(F32), axis=0)


def pieces(value):
    high = lax.reduce_precision(value, 8, 7)
    rest = value - high
    middle = lax.reduce_precision(rest, 8, 7)
    return [p.astype(BF) for p in (high, middle, rest - middle)]


def columns(*values):
    return jnp.stack([p for v in values for p in pieces(v)], axis=-1)


def column(lanes, index):
    return jnp.sum(lanes[..., 3 * index : 3 * index + 3].astype(F32), axis=-1)


def swap(value, axis, bits):
    return lax.ppermute(value, axis, [(i, i ^ bits) for i in range(lax.axis_size(axis))])


def other_core(value):
    return swap(value, "co", 1)


def dot(a, b, contract):
    return lax.dot_general(a, b, ((contract[:1], contract[1:]), ((), ())), preferred_element_type=F32)


VMEM = pl.BlockSpec(memory_space=pltpu.VMEM)


def local_call(kernel, out, *args, scratch=(), scalar=False):
    specs = [VMEM] * len(args)
    if scalar:
        specs[0] = pl.BlockSpec(memory_space=pltpu.SMEM)
    return pl.pallas_call(
        kernel,
        out_shape=out,
        in_specs=specs,
        out_specs=jax.tree.map(lambda _: VMEM, out),
        scratch_shapes=scratch,
        compiler_params=pltpu.CompilerParams(vmem_limit_bytes=40 * 1024 * 1024),
    )(*args)


def fill_kernel(y_ref, both_ref, up_ref, down_ref, extra_ref, out_ref):
    n, block, _ = out_ref.shape
    local, hid = up_ref.shape
    part = jnp.dot(y_ref[...], up_ref[...], preferred_element_type=F32).astype(BF)
    out_ref[:, :, :hid] = part.reshape(n, block, hid)
    part = dot(both_ref[:, local:], down_ref[...], (1, 1)).astype(BF)
    out_ref[:, :, hid : 2 * hid] = part.reshape(n, block, hid)
    out_ref[:, :, 2 * hid :] = extra_ref[...]


def lane_pieces(values, lane):
    out = jnp.zeros(lane.shape, F32)
    for i, value in enumerate(values):
        for j in range(3):
            piece = value.astype(BF).astype(F32)
            out = jnp.where(lane == 3 * i + j, piece, out)
            value = value - piece
    return out


def tokens_kernel(acts_ref, both_ref, up_ref, tilt_ref, gain_ref, tail_ref, z_ref):
    n, high, _ = tail_ref.shape
    local, hid = up_ref.shape
    tall = acts_ref.shape[0]
    rows = tall // n
    grad = acts_ref[:, hid : 2 * hid]
    marks = acts_ref[:, 2 * hid :].astype(F32)
    lane = lax.broadcasted_iota(jnp.int32, marks.shape, 1)

    def taken(index):
        mine = (lane >= 3 * index) & (lane < 3 * index + 3)
        return jnp.sum(jnp.where(mine, marks, 0.0), axis=1, keepdims=True)

    cross, mean, inv = (taken(i) for i in range(3))
    normed = (both_ref[:, :local].astype(F32) - mean) * inv
    z_ref[...] = (normed * gain_ref[...]).astype(BF)
    d_z = dot(grad, up_ref[...], (1, 1))
    level = jnp.sum(grad.astype(F32) * tilt_ref[...], axis=1, keepdims=True)
    tail_ref[:, :rows, :local] = d_z.astype(BF).reshape(n, rows, local)
    sums = lane_pieces((level, cross), lane).astype(BF)
    tail_ref[:, :rows, local:] = sums.reshape(n, rows, LANES)
    rest = jnp.sum(d_z * normed, axis=0, keepdims=True)
    row = lax.broadcasted_iota(jnp.int32, (high - rows, local), 0)
    gains = jnp.zeros(row.shape, F32)
    for j in range(3):
        piece = rest.astype(BF).astype(F32)
        gains = jnp.where(row == j, piece, gains)
        rest = rest - piece
    gains = gains.astype(BF)
    for i in range(n):
        tail_ref[i, rows:, :local] = gains
        tail_ref[i, rows:, local:] = jnp.zeros((high - rows, LANES), BF)


def grads_kernel(core_ref, acts_ref, both_ref, z_ref, keep_ref, give_ref, down_ref, up_ref):
    hid, local = down_ref.shape
    down_ref[...] = dot(acts_ref[:, :hid], both_ref[:, local:], (0, 0)).astype(BF)
    up_ref[...] = dot(z_ref[...], acts_ref[:, hid : 2 * hid], (0, 0)).astype(BF)
    core = core_ref[0]
    n = keep_ref.shape[0]
    for ref, which in ((keep_ref, core), (give_ref, 1 - core)):
        for j in range(n):
            first = 0
            for whole in (down_ref, up_ref):
                height = whole.shape[0] // (2 * n)
                start = pl.multiple_of((2 * j + which) * height, 16)
                for i in range(0, whole.shape[1], LANES):
                    ref[j, first : first + height, :] = whole[pl.ds(start, height), i : i + LANES]
                    first += height


def merge_kernel(*refs):
    *parts, down_ref, up_ref = refs
    first = 0
    for out in (down_ref, up_ref):
        height = out.shape[0]
        for i in range(0, out.shape[1], LANES):
            total = sum(p[first : first + height, :].astype(F32) for p in parts)
            out[:, i : i + LANES] = total.astype(BF)
            first += height


def body(x_in, gain, w_up, w_down, d_out):
    rows, local = x_in.shape
    n_gx, n_yl, n_gz = (lax.axis_size(a) for a in ("gx", "yl", GZ))
    width = local * n_gz
    up_rows, hid = w_up.shape
    down_rows = w_down.shape[0]
    all_rows = rows * n_gx
    block = all_rows // n_gz
    even = lax.axis_index("co") == 0

    def by_core(mine, other):
        pair = [jnp.where(even, mine, other), jnp.where(even, other, mine)]
        return jnp.stack(pair, axis=1).reshape(-1, mine.shape[-1])

    down_full = lax.all_gather(w_down, GY, axis=0, tiled=True)
    up_mine = spread(w_up, "yl")
    both = lax.all_gather(jnp.concatenate([x_in, d_out], axis=1), "gx", axis=0, tiled=True)
    both, up_mine = lax.optimization_barrier((both, up_mine))
    up_full = by_core(up_mine, other_core(up_mine))
    x_rows = both[:, :local].astype(F32)

    part_sum = jnp.sum(x_rows, axis=1)
    off = x_rows - (part_sum / local)[:, None]
    second = jnp.sum(off * off, axis=1)
    y = (off * gain).astype(BF)
    gains = jnp.pad(jnp.stack(pieces(gain)), ((0, 5), (0, 0)))
    tilt = jnp.sum(dot(gains, up_full, (1, 0)), axis=0)
    tilt = jnp.stack(pieces(tilt)).reshape(3 * n_gz, -1)
    spare = LANES - tilt.shape[1]
    tilt = jnp.pad(tilt, ((0, block - tilt.shape[0]), (0, 0)))
    marks = columns(part_sum, second)
    extra = jnp.concatenate(
        [
            jnp.pad(marks, ((0, 0), (0, spare - marks.shape[1]))).reshape(n_gz, block, spare),
            jnp.broadcast_to(tilt, (n_gz, *tilt.shape)),
        ],
        axis=2,
    )
    pair = local_call(
        fill_kernel,
        jax.ShapeDtypeStruct((n_gz, block, 2 * hid + LANES), BF),
        *(y, both, up_full, down_full, extra),
    )
    pair = exchange(pair, GZ)
    marks = pair[:, :, 2 * hid : 2 * hid + spare]
    tilts = pair[:, : 3 * n_gz, 2 * hid + spare :].astype(F32)
    tilts = jnp.sum(tilts.reshape(n_gz, 3, n_gz, -1), axis=1).reshape(n_gz, hid)
    means = column(marks, 0) / local
    mean = jnp.sum(means, axis=0) / n_gz
    shift = means - mean
    var = (jnp.sum(column(marks, 1), axis=0) + local * jnp.sum(shift * shift, axis=0)) / width
    inv = lax.rsqrt(var + 1e-05)
    hidden = summed(pair[:, :, :hid]) + sum(
        shift[i][:, None] * tilts[i][None] for i in range(n_gz)
    )
    hidden = hidden * inv[:, None]
    d_act = summed(pair[:, :, hid : 2 * hid])
    act_f, slope = gelu_pair(hidden)
    d_hidden = (d_act * slope).astype(BF)
    cross = jnp.sum(d_hidden.astype(F32) * hidden, axis=1)
    marks = columns(cross, mean, inv)
    marks = jnp.pad(marks, ((0, 0), (0, LANES - marks.shape[1])))
    acts = jnp.concatenate([act_f.astype(BF), d_hidden, marks], axis=1)
    acts = spread(acts, GZ).reshape(all_rows, -1)
    _, mean, inv = (column(acts[:, 2 * hid :], i) for i in range(3))

    tail, z = local_call(
        tokens_kernel,
        (
            jax.ShapeDtypeStruct((n_gx, rows + 8, local + LANES), BF),
            jax.ShapeDtypeStruct((all_rows, local), BF),
        ),
        *(acts, both, up_full, jnp.sum(tilts, axis=0)[None], gain[None]),
    )
    tail = exchange(tail, "gx")

    packed = down_rows * (local // LANES) + up_rows * (hid // LANES)
    keep, give = local_call(
        grads_kernel,
        (jax.ShapeDtypeStruct((n_yl, packed, LANES), BF),) * 2,
        *(lax.axis_index("co")[None], acts, both, z),
        scratch=(pltpu.VMEM((hid, local), BF), pltpu.VMEM((local, hid), BF)),
        scalar=True,
    )
    grads = (keep.astype(F32) + other_core(give).astype(F32)).astype(BF)
    place = lax.axis_index("yl")

    def part(index):
        return lax.dynamic_index_in_dim(grads, index, keepdims=False)

    grads = [part(place)] + [swap(part(place ^ k), "yl", k) for k in range(1, n_yl)]
    d_z = summed(tail[:, :rows, :local])
    marks = summed(tail[:, :rows, local:])
    scaled_sum, cross_sum = (column(marks, i)[:, None] / width for i in range(2))
    d_gain = jnp.sum(tail[:, rows : rows + 3, :local].astype(F32), axis=(0, 1))
    for axis, bits in (("yl", 1), ("yl", 2), ("co", 1)):
        d_gain = d_gain + swap(d_gain, axis, bits)

    d_w_down, d_w_up = local_call(
        merge_kernel,
        (
            jax.ShapeDtypeStruct((down_rows, local), BF),
            jax.ShapeDtypeStruct((up_rows, hid), BF),
        ),
        *grads,
    )

    first = lax.axis_index("gx") * rows

    def own(values):
        return lax.dynamic_slice(values, (first,), (rows,))[:, None]

    own_inv = own(inv)
    own_normed = (x_in.astype(F32) - own(mean)) * own_inv
    d_x = own_inv * (d_z * gain - scaled_sum - own_normed * cross_sum)
    return (d_x.astype(BF), d_w_up, d_w_down, d_gain)


def solution(mesh):
    sizes = mesh.shape
    cores, x_chips = 2, sizes["gz"] // 2
    fine = Mesh(
        mesh.devices.reshape(sizes["gx"], sizes["gy"] // cores, cores, 2, x_chips),
        ("gx", *GY, *GZ),
    )
    placed = (
        P((*GY, "gx"), GZ),
        P(GZ),
        P((*GZ, *GY), "gx"),
        P(("gx", *GY), GZ),
        P((*GY, "gx"), GZ),
    )
    return jax.shard_map(
        body,
        mesh=fine,
        in_specs=placed,
        out_specs=(P((*GY, "gx"), GZ), P((*GZ, *GY), "gx"), P(("gx", *GY), GZ), P(GZ)),
        check_vma=False,
    )
```

```python
import jax
import jax.numpy as jnp
from jax import lax
from jax.experimental import pallas as pl
from jax.experimental.pallas import tpu as pltpu
from jax.sharding import Mesh
from jax.sharding import PartitionSpec as P

BF, F32 = jnp.bfloat16, jnp.float32
LANES = 128
GY, GZ = ("yl", "co"), ("yh", "xx")


def gelu_pair(hidden):
    cdf = 0.5 * (1.0 + jax.scipy.special.erf(hidden * 0.7071067811865476))
    slope = cdf + hidden * jnp.exp(-0.5 * hidden * hidden) * 0.3989422804014327
    return (hidden * cdf, slope)


def exchange(blocks, axis):
    return lax.all_to_all(blocks, axis, 0, 0, tiled=True)


def spread(value, axis):
    n = lax.axis_size(axis)
    return exchange(jnp.broadcast_to(value[None], (n, *value.shape)), axis)


def summed(blocks):
    return jnp.sum(blocks.astype(F32), axis=0)


def pieces(value):
    high = lax.reduce_precision(value, 8, 7)
    rest = value - high
    middle = lax.reduce_precision(rest, 8, 7)
    return [p.astype(BF) for p in (high, middle, rest - middle)]


def columns(*values):
    return jnp.stack([p for v in values for p in pieces(v)], axis=-1)


def column(lanes, index):
    return jnp.sum(lanes[..., 3 * index : 3 * index + 3].astype(F32), axis=-1)


def swap(value, axis, bits):
    return lax.ppermute(value, axis, [(i, i ^ bits) for i in range(lax.axis_size(axis))])


def other_core(value):
    return swap(value, "co", 1)


def dot(a, b, contract):
    return lax.dot_general(a, b, ((contract[:1], contract[1:]), ((), ())), preferred_element_type=F32)


VMEM = pl.BlockSpec(memory_space=pltpu.VMEM)


def local_call(kernel, out, *args, scratch=(), scalar=False):
    specs = [VMEM] * len(args)
    if scalar:
        specs[0] = pl.BlockSpec(memory_space=pltpu.SMEM)
    return pl.pallas_call(
        kernel,
        out_shape=out,
        in_specs=specs,
        out_specs=jax.tree.map(lambda _: VMEM, out),
        scratch_shapes=scratch,
        compiler_params=pltpu.CompilerParams(vmem_limit_bytes=40 * 1024 * 1024),
    )(*args)


def fill_kernel(y_ref, both_ref, up_ref, down_ref, extra_ref, out_ref):
    n, block, _ = out_ref.shape
    local, hid = up_ref.shape
    part = jnp.dot(y_ref[...], up_ref[...], preferred_element_type=F32).astype(BF)
    out_ref[:, :, :hid] = part.reshape(n, block, hid)
    part = dot(both_ref[:, local:], down_ref[...], (1, 1)).astype(BF)
    out_ref[:, :, hid : 2 * hid] = part.reshape(n, block, hid)
    out_ref[:, :, 2 * hid :] = extra_ref[...]


def lane_pieces(values, lane):
    out = jnp.zeros(lane.shape, F32)
    for i, value in enumerate(values):
        for j in range(3):
            piece = value.astype(BF).astype(F32)
            out = jnp.where(lane == 3 * i + j, piece, out)
            value = value - piece
    return out


def halves(index, own_ref, peer_ref):
    tall = own_ref.shape[0]
    for ref, which in ((own_ref, index), (peer_ref, 1 - index)):
        yield ref, which, pl.ds(pl.multiple_of(which * tall, 16), tall)


def tokens_kernel(
    place_ref, own_ref, peer_ref, both_ref, up_ref, tilt_ref, gain_ref, tail_ref, z_ref, stats_ref
):
    n, high, _ = tail_ref.shape
    local, hid = up_ref.shape
    rows = both_ref.shape[0] // n
    rest = 0.0
    for ref, which, span in halves(place_ref[1], own_ref, peer_ref):
        grad = ref[:, hid : 2 * hid]
        marks = ref[:, 2 * hid :].astype(F32)
        lane = lax.broadcasted_iota(jnp.int32, marks.shape, 1)

        def taken(index):
            mine = (lane >= 3 * index) & (lane < 3 * index + 3)
            return jnp.sum(jnp.where(mine, marks, 0.0), axis=1, keepdims=True)

        cross, mean, inv = (taken(i) for i in range(3))
        stats_ref[span, :] = jnp.where(lane == 0, mean, inv)
        normed = (both_ref[span, :local].astype(F32) - mean) * inv
        z_ref[span, :] = (normed * gain_ref[...]).astype(BF)
        d_z = dot(grad, up_ref[...], (1, 1))
        level = jnp.sum(grad.astype(F32) * tilt_ref[...], axis=1, keepdims=True)
        blocks = pl.ds(which * (n // 2), n // 2)
        tail_ref[blocks, :rows, :local] = d_z.astype(BF).reshape(n // 2, rows, local)
        sums = lane_pieces((level, cross), lane).astype(BF)
        tail_ref[blocks, :rows, local:] = sums.reshape(n // 2, rows, LANES)
        rest = rest + jnp.sum(d_z * normed, axis=0, keepdims=True)
    row = lax.broadcasted_iota(jnp.int32, (high - rows, local), 0)
    gains = jnp.zeros(row.shape, F32)
    for j in range(3):
        piece = rest.astype(BF).astype(F32)
        gains = jnp.where(row == j, piece, gains)
        rest = rest - piece
    gains = gains.astype(BF)
    for i in range(n):
        tail_ref[i, rows:, :local] = gains
        tail_ref[i, rows:, local:] = jnp.zeros((high - rows, LANES), BF)


def grads_kernel(
    place_ref, own_ref, peer_ref, both_ref, z_ref, keep_ref, give_ref, down_ref, up_ref
):
    hid, local = down_ref.shape
    down, up = 0.0, 0.0
    for ref, _, span in halves(place_ref[1], own_ref, peer_ref):
        down = down + dot(ref[:, :hid], both_ref[span, local:], (0, 0))
        up = up + dot(z_ref[span, :], ref[:, hid : 2 * hid], (0, 0))
    down_ref[...] = down.astype(BF)
    up_ref[...] = up.astype(BF)
    core = place_ref[0]
    n = keep_ref.shape[0]
    for ref, which in ((keep_ref, core), (give_ref, 1 - core)):
        for j in range(n):
            first = 0
            for whole in (down_ref, up_ref):
                height = whole.shape[0] // (2 * n)
                start = pl.multiple_of((2 * j + which) * height, 16)
                for i in range(0, whole.shape[1], LANES):
                    ref[j, first : first + height, :] = whole[pl.ds(start, height), i : i + LANES]
                    first += height


def merge_kernel(*refs):
    *parts, down_ref, up_ref = refs
    first = 0
    for out in (down_ref, up_ref):
        height = out.shape[0]
        for i in range(0, out.shape[1], LANES):
            total = sum(p[first : first + height, :].astype(F32) for p in parts)
            out[:, i : i + LANES] = total.astype(BF)
            first += height


def body(x_in, gain, w_up, w_down, d_out):
    rows, local = x_in.shape
    n_gx, n_yl, n_gz = (lax.axis_size(a) for a in ("gx", "yl", GZ))
    width = local * n_gz
    up_rows, hid = w_up.shape
    down_rows = w_down.shape[0]
    all_rows = rows * n_gx
    block = all_rows // n_gz
    even = lax.axis_index("co") == 0

    def by_core(mine, other):
        pair = [jnp.where(even, mine, other), jnp.where(even, other, mine)]
        return jnp.stack(pair, axis=1).reshape(-1, mine.shape[-1])

    down_full = lax.all_gather(w_down, GY, axis=0, tiled=True)
    up_mine = spread(w_up, "yl")
    both = lax.all_gather(jnp.concatenate([x_in, d_out], axis=1), "gx", axis=0, tiled=True)
    both, up_mine = lax.optimization_barrier((both, up_mine))
    up_full = by_core(up_mine, other_core(up_mine))
    x_rows = both[:, :local].astype(F32)

    part_sum = jnp.sum(x_rows, axis=1)
    off = x_rows - (part_sum / local)[:, None]
    second = jnp.sum(off * off, axis=1)
    y = (off * gain).astype(BF)
    gains = jnp.pad(jnp.stack(pieces(gain)), ((0, 5), (0, 0)))
    tilt = jnp.sum(dot(gains, up_full, (1, 0)), axis=0)
    tilt = jnp.stack(pieces(tilt)).reshape(3 * n_gz, -1)
    spare = LANES - tilt.shape[1]
    tilt = jnp.pad(tilt, ((0, block - tilt.shape[0]), (0, 0)))
    marks = columns(part_sum, second)
    extra = jnp.concatenate(
        [
            jnp.pad(marks, ((0, 0), (0, spare - marks.shape[1]))).reshape(n_gz, block, spare),
            jnp.broadcast_to(tilt, (n_gz, *tilt.shape)),
        ],
        axis=2,
    )
    pair = local_call(
        fill_kernel,
        jax.ShapeDtypeStruct((n_gz, block, 2 * hid + LANES), BF),
        *(y, both, up_full, down_full, extra),
    )
    pair = exchange(pair, GZ)
    marks = pair[:, :, 2 * hid : 2 * hid + spare]
    tilts = pair[:, : 3 * n_gz, 2 * hid + spare :].astype(F32)
    tilts = jnp.sum(tilts.reshape(n_gz, 3, n_gz, -1), axis=1).reshape(n_gz, hid)
    means = column(marks, 0) / local
    mean = jnp.sum(means, axis=0) / n_gz
    shift = means - mean
    var = (jnp.sum(column(marks, 1), axis=0) + local * jnp.sum(shift * shift, axis=0)) / width
    inv = lax.rsqrt(var + 1e-05)
    hidden = summed(pair[:, :, :hid]) + sum(
        shift[i][:, None] * tilts[i][None] for i in range(n_gz)
    )
    hidden = hidden * inv[:, None]
    d_act = summed(pair[:, :, hid : 2 * hid])
    act_f, slope = gelu_pair(hidden)
    d_hidden = (d_act * slope).astype(BF)
    cross = jnp.sum(d_hidden.astype(F32) * hidden, axis=1)
    marks = columns(cross, mean, inv)
    marks = jnp.pad(marks, ((0, 0), (0, LANES - marks.shape[1])))
    acts = jnp.concatenate([act_f.astype(BF), d_hidden, marks], axis=1)
    peer = swap(acts, "yh", 1)
    own = spread(acts, "xx")
    own, peer = lax.optimization_barrier((own, peer))
    own, peer = (v.reshape(all_rows // 2, -1) for v in (own, spread(peer, "xx")))

    place = jnp.stack([lax.axis_index("co"), lax.axis_index("yh")])
    tail, z, stats = local_call(
        tokens_kernel,
        (
            jax.ShapeDtypeStruct((n_gx, rows + 8, local + LANES), BF),
            jax.ShapeDtypeStruct((all_rows, local), BF),
            jax.ShapeDtypeStruct((all_rows, LANES), F32),
        ),
        *(place, own, peer, both, up_full, jnp.sum(tilts, axis=0)[None], gain[None]),
        scalar=True,
    )
    tail = exchange(tail, "gx")

    packed = down_rows * (local // LANES) + up_rows * (hid // LANES)
    keep, give = local_call(
        grads_kernel,
        (jax.ShapeDtypeStruct((n_yl, packed, LANES), BF),) * 2,
        *(place, own, peer, both, z),
        scratch=(pltpu.VMEM((hid, local), BF), pltpu.VMEM((local, hid), BF)),
        scalar=True,
    )
    grads = (keep.astype(F32) + other_core(give).astype(F32)).astype(BF)
    turn = lax.axis_index("yl")

    def part(index):
        return lax.dynamic_index_in_dim(grads, index, keepdims=False)

    grads = [part(turn)] + [swap(part(turn ^ k), "yl", k) for k in range(1, n_yl)]
    d_z = summed(tail[:, :rows, :local])
    marks = summed(tail[:, :rows, local:])
    scaled_sum, cross_sum = (column(marks, i)[:, None] / width for i in range(2))
    d_gain = jnp.sum(tail[:, rows : rows + 3, :local].astype(F32), axis=(0, 1))
    for axis, bits in (("yl", 1), ("yl", 2), ("co", 1)):
        d_gain = d_gain + swap(d_gain, axis, bits)

    d_w_down, d_w_up = local_call(
        merge_kernel,
        (
            jax.ShapeDtypeStruct((down_rows, local), BF),
            jax.ShapeDtypeStruct((up_rows, hid), BF),
        ),
        *grads,
    )

    first = lax.axis_index("gx") * rows

    stats = lax.dynamic_slice(stats, (first, 0), (rows, 2))
    own_inv = stats[:, 1:]
    own_normed = (x_in.astype(F32) - stats[:, :1]) * own_inv
    d_x = own_inv * (d_z * gain - scaled_sum - own_normed * cross_sum)
    return (d_x.astype(BF), d_w_up, d_w_down, d_gain)


def solution(mesh):
    sizes = mesh.shape
    cores, x_chips = 2, sizes["gz"] // 2
    fine = Mesh(
        mesh.devices.reshape(sizes["gx"], sizes["gy"] // cores, cores, 2, x_chips),
        ("gx", *GY, *GZ),
    )
    placed = (
        P((*GY, "gx"), GZ),
        P(GZ),
        P((*GZ, *GY), "gx"),
        P(("gx", *GY), GZ),
        P((*GY, "gx"), GZ),
    )
    return jax.shard_map(
        body,
        mesh=fine,
        in_specs=placed,
        out_specs=(P((*GY, "gx"), GZ), P((*GZ, *GY), "gx"), P(("gx", *GY), GZ), P(GZ)),
        check_vma=False,
    )
```

```python
import jax
import jax.numpy as jnp
from jax import lax
from jax.experimental import pallas as pl
from jax.experimental.pallas import tpu as pltpu
from jax.sharding import Mesh
from jax.sharding import PartitionSpec as P

BF, F32 = jnp.bfloat16, jnp.float32
LANES = 128
GY, GZ = ("yl", "co"), ("yh", "xx")


def gelu_pair(hidden):
    cdf = 0.5 * (1.0 + jax.scipy.special.erf(hidden * 0.7071067811865476))
    slope = cdf + hidden * jnp.exp(-0.5 * hidden * hidden) * 0.3989422804014327
    return (hidden * cdf, slope)


def exchange(blocks, axis):
    return lax.all_to_all(blocks, axis, 0, 0, tiled=True)


def spread(value, axis):
    n = lax.axis_size(axis)
    return exchange(jnp.broadcast_to(value[None], (n, *value.shape)), axis)


def summed(blocks):
    return jnp.sum(blocks.astype(F32), axis=0)


def pieces(value):
    high = lax.reduce_precision(value, 8, 7)
    rest = value - high
    middle = lax.reduce_precision(rest, 8, 7)
    return [p.astype(BF) for p in (high, middle, rest - middle)]


def columns(*values):
    return jnp.stack([p for v in values for p in pieces(v)], axis=-1)


def column(lanes, index):
    return jnp.sum(lanes[..., 3 * index : 3 * index + 3].astype(F32), axis=-1)


def swap(value, axis, bits):
    return lax.ppermute(value, axis, [(i, i ^ bits) for i in range(lax.axis_size(axis))])


def other_core(value):
    return swap(value, "co", 1)


def dot(a, b, contract):
    return lax.dot_general(a, b, ((contract[:1], contract[1:]), ((), ())), preferred_element_type=F32)


VMEM = pl.BlockSpec(memory_space=pltpu.VMEM)


def local_call(kernel, out, *args, scratch=(), scalar=False):
    specs = [VMEM] * len(args)
    if scalar:
        specs[0] = pl.BlockSpec(memory_space=pltpu.SMEM)
    return pl.pallas_call(
        kernel,
        out_shape=out,
        in_specs=specs,
        out_specs=jax.tree.map(lambda _: VMEM, out),
        scratch_shapes=scratch,
        compiler_params=pltpu.CompilerParams(vmem_limit_bytes=40 * 1024 * 1024),
    )(*args)


def fill_kernel(y_ref, both_ref, up_ref, down_ref, extra_ref, out_ref):
    n, block, _ = out_ref.shape
    local, hid = up_ref.shape
    part = jnp.dot(y_ref[...], up_ref[...], preferred_element_type=F32).astype(BF)
    out_ref[:, :, :hid] = part.reshape(n, block, hid)
    part = dot(both_ref[:, local:], down_ref[...], (1, 1)).astype(BF)
    out_ref[:, :, hid : 2 * hid] = part.reshape(n, block, hid)
    out_ref[:, :, 2 * hid :] = extra_ref[...]


def lane_pieces(values, lane):
    out = jnp.zeros(lane.shape, F32)
    for i, value in enumerate(values):
        for j in range(3):
            piece = value.astype(BF).astype(F32)
            out = jnp.where(lane == 3 * i + j, piece, out)
            value = value - piece
    return out


def halves(index, own_ref, peer_ref):
    tall = own_ref.shape[0]
    for ref, which in ((own_ref, index), (peer_ref, 1 - index)):
        yield ref, which, pl.ds(pl.multiple_of(which * tall, 16), tall)


def tokens_kernel(
    place_ref, own_ref, peer_ref, both_ref, up_ref, tilt_ref, gain_ref, tail_ref, z_ref, stats_ref
):
    n, high, _ = tail_ref.shape
    local, hid = up_ref.shape
    rows = both_ref.shape[0] // n
    rest = 0.0
    for ref, which, span in halves(place_ref[1], own_ref, peer_ref):
        grad = ref[:, hid : 2 * hid]
        marks = ref[:, 2 * hid :].astype(F32)
        lane = lax.broadcasted_iota(jnp.int32, marks.shape, 1)

        def taken(index):
            mine = (lane >= 3 * index) & (lane < 3 * index + 3)
            return jnp.sum(jnp.where(mine, marks, 0.0), axis=1, keepdims=True)

        cross, mean, inv = (taken(i) for i in range(3))
        stats_ref[span, :] = jnp.where(lane == 0, mean, inv)
        normed = (both_ref[span, :local].astype(F32) - mean) * inv
        z_ref[span, :] = (normed * gain_ref[...]).astype(BF)
        d_z = dot(grad, up_ref[...], (1, 1))
        level = jnp.sum(grad.astype(F32) * tilt_ref[...], axis=1, keepdims=True)
        blocks = pl.ds(which * (n // 2), n // 2)
        tail_ref[blocks, :rows, :local] = d_z.astype(BF).reshape(n // 2, rows, local)
        sums = lane_pieces((level, cross), lane).astype(BF)
        tail_ref[blocks, :rows, local:] = sums.reshape(n // 2, rows, LANES)
        rest = rest + jnp.sum(d_z * normed, axis=0, keepdims=True)
    row = lax.broadcasted_iota(jnp.int32, (high - rows, local), 0)
    gains = jnp.zeros(row.shape, F32)
    for j in range(3):
        piece = rest.astype(BF).astype(F32)
        gains = jnp.where(row == j, piece, gains)
        rest = rest - piece
    gains = gains.astype(BF)
    for i in range(n):
        tail_ref[i, rows:, :local] = gains
        tail_ref[i, rows:, local:] = jnp.zeros((high - rows, LANES), BF)


def grads_kernel(
    place_ref, own_ref, peer_ref, both_ref, z_ref, keep_ref, give_ref, down_ref, up_ref
):
    hid, local = down_ref.shape
    down, up = 0.0, 0.0
    for ref, _, span in halves(place_ref[1], own_ref, peer_ref):
        down = down + dot(ref[:, :hid], both_ref[span, local:], (0, 0))
        up = up + dot(z_ref[span, :], ref[:, hid : 2 * hid], (0, 0))
    down_ref[...] = down.astype(BF)
    up_ref[...] = up.astype(BF)
    core = place_ref[0]
    n = keep_ref.shape[0]
    for ref, which in ((keep_ref, core), (give_ref, 1 - core)):
        for j in range(n):
            first = 0
            for whole in (down_ref, up_ref):
                height = whole.shape[0] // (2 * n)
                start = pl.multiple_of((2 * j + which) * height, 16)
                for i in range(0, whole.shape[1], LANES):
                    ref[j, first : first + height, :] = whole[pl.ds(start, height), i : i + LANES]
                    first += height


def merge_kernel(*refs):
    *parts, down_ref, up_ref = refs
    first = 0
    for out in (down_ref, up_ref):
        height = out.shape[0]
        for i in range(0, out.shape[1], LANES):
            total = sum(p[first : first + height, :].astype(F32) for p in parts)
            out[:, i : i + LANES] = total.astype(BF)
            first += height


def body(x_in, gain, w_up, w_down, d_out):
    rows, local = x_in.shape
    n_gx, n_yl, n_gz = (lax.axis_size(a) for a in ("gx", "yl", GZ))
    width = local * n_gz
    up_rows, hid = w_up.shape
    down_rows = w_down.shape[0]
    all_rows = rows * n_gx
    block = all_rows // n_gz
    even = lax.axis_index("co") == 0

    def by_core(mine, other):
        pair = [jnp.where(even, mine, other), jnp.where(even, other, mine)]
        return jnp.stack(pair, axis=1).reshape(-1, mine.shape[-1])

    down_full = lax.all_gather(w_down, GY, axis=0, tiled=True)
    up_mine = spread(w_up, "yl")
    both = lax.all_gather(jnp.concatenate([x_in, d_out], axis=1), "gx", axis=0, tiled=True)
    both, up_mine = lax.optimization_barrier((both, up_mine))
    up_full = by_core(up_mine, other_core(up_mine))
    x_rows = both[:, :local].astype(F32)

    part_sum = jnp.sum(x_rows, axis=1)
    off = x_rows - (part_sum / local)[:, None]
    second = jnp.sum(off * off, axis=1)
    y = (off * gain).astype(BF)
    gains = jnp.pad(jnp.stack(pieces(gain)), ((0, 5), (0, 0)))
    tilt = jnp.sum(dot(gains, up_full, (1, 0)), axis=0)
    tilt = jnp.stack(pieces(tilt)).reshape(3 * n_gz, -1)
    spare = LANES - tilt.shape[1]
    tilt = jnp.pad(tilt, ((0, block - tilt.shape[0]), (0, 0)))
    marks = columns(part_sum, second)
    extra = jnp.concatenate(
        [
            jnp.pad(marks, ((0, 0), (0, spare - marks.shape[1]))).reshape(n_gz, block, spare),
            jnp.broadcast_to(tilt, (n_gz, *tilt.shape)),
        ],
        axis=2,
    )
    pair = local_call(
        fill_kernel,
        jax.ShapeDtypeStruct((n_gz, block, 2 * hid + LANES), BF),
        *(y, both, up_full, down_full, extra),
    )
    pair = exchange(pair, GZ)
    marks = pair[:, :, 2 * hid : 2 * hid + spare]
    tilts = pair[:, : 3 * n_gz, 2 * hid + spare :].astype(F32)
    tilts = jnp.sum(tilts.reshape(n_gz, 3, n_gz, -1), axis=1).reshape(n_gz, hid)
    means = column(marks, 0) / local
    mean = jnp.sum(means, axis=0) / n_gz
    shift = means - mean
    var = (jnp.sum(column(marks, 1), axis=0) + local * jnp.sum(shift * shift, axis=0)) / width
    inv = lax.rsqrt(var + 1e-05)
    hidden = summed(pair[:, :, :hid]) + sum(
        shift[i][:, None] * tilts[i][None] for i in range(n_gz)
    )
    hidden = hidden * inv[:, None]
    d_act = summed(pair[:, :, hid : 2 * hid])
    act_f, slope = gelu_pair(hidden)
    d_hidden = (d_act * slope).astype(BF)
    cross = jnp.sum(d_hidden.astype(F32) * hidden, axis=1)
    marks = columns(cross, mean, inv)
    marks = jnp.pad(marks, ((0, 0), (0, LANES - marks.shape[1])))
    acts = jnp.concatenate([act_f.astype(BF), d_hidden, marks], axis=1)
    peer = swap(acts, "yh", 1)
    own = spread(acts, "xx")
    own, peer = lax.optimization_barrier((own, peer))
    own, peer = (v.reshape(all_rows // 2, -1) for v in (own, spread(peer, "xx")))

    place = jnp.stack([lax.axis_index("co"), lax.axis_index("yh")])
    tail, z, stats = local_call(
        tokens_kernel,
        (
            jax.ShapeDtypeStruct((n_gx, rows + 8, local + LANES), BF),
            jax.ShapeDtypeStruct((all_rows, local), BF),
            jax.ShapeDtypeStruct((all_rows, LANES), F32),
        ),
        *(place, own, peer, both, up_full, jnp.sum(tilts, axis=0)[None], gain[None]),
        scalar=True,
    )
    tail = exchange(tail, "gx")

    packed = down_rows * (local // LANES) + up_rows * (hid // LANES)
    keep, give = local_call(
        grads_kernel,
        (jax.ShapeDtypeStruct((n_yl, packed, LANES), BF),) * 2,
        *(place, own, peer, both, z),
        scratch=(pltpu.VMEM((hid, local), BF), pltpu.VMEM((local, hid), BF)),
        scalar=True,
    )
    grads = (keep.astype(F32) + other_core(give).astype(F32)).astype(BF)
    turn = lax.axis_index("yl")

    def part(index):
        return lax.dynamic_index_in_dim(grads, index, keepdims=False)

    grads = [part(turn)] + [swap(part(turn ^ k), "yl", k) for k in range(1, n_yl)]
    d_z = summed(tail[:, :rows, :local])
    marks = summed(tail[:, :rows, local:])
    scaled_sum, cross_sum = (column(marks, i)[:, None] / width for i in range(2))
    d_gain = jnp.sum(tail[:, rows : rows + 3, :local].astype(F32), axis=(0, 1))
    d_gain = jnp.sum(lax.all_gather(d_gain.reshape(-1, LANES), GY), axis=0).reshape(-1)

    d_w_down, d_w_up = local_call(
        merge_kernel,
        (
            jax.ShapeDtypeStruct((down_rows, local), BF),
            jax.ShapeDtypeStruct((up_rows, hid), BF),
        ),
        *grads,
    )

    first = lax.axis_index("gx") * rows

    stats = lax.dynamic_slice(stats, (first, 0), (rows, 2))
    own_inv = stats[:, 1:]
    own_normed = (x_in.astype(F32) - stats[:, :1]) * own_inv
    d_x = own_inv * (d_z * gain - scaled_sum - own_normed * cross_sum)
    return (d_x.astype(BF), d_w_up, d_w_down, d_gain)


def solution(mesh):
    sizes = mesh.shape
    cores, x_chips = 2, sizes["gz"] // 2
    fine = Mesh(
        mesh.devices.reshape(sizes["gx"], sizes["gy"] // cores, cores, 2, x_chips),
        ("gx", *GY, *GZ),
    )
    placed = (
        P((*GY, "gx"), GZ),
        P(GZ),
        P((*GZ, *GY), "gx"),
        P(("gx", *GY), GZ),
        P((*GY, "gx"), GZ),
    )
    return jax.shard_map(
        body,
        mesh=fine,
        in_specs=placed,
        out_specs=(P((*GY, "gx"), GZ), P((*GZ, *GY), "gx"), P(("gx", *GY), GZ), P(GZ)),
        check_vma=False,
    )
```

```python
import jax
import jax.numpy as jnp
from jax import lax
from jax.experimental import pallas as pl
from jax.experimental.pallas import tpu as pltpu
from jax.sharding import Mesh
from jax.sharding import PartitionSpec as P

BF, F32 = jnp.bfloat16, jnp.float32
LANES = 128
GY, GZ = ("yl", "co"), ("yh", "xx")


def gelu_pair(hidden):
    cdf = 0.5 * (1.0 + jax.scipy.special.erf(hidden * 0.7071067811865476))
    slope = cdf + hidden * jnp.exp(-0.5 * hidden * hidden) * 0.3989422804014327
    return (hidden * cdf, slope)


def exchange(blocks, axis):
    return lax.all_to_all(blocks, axis, 0, 0, tiled=True)


def spread(value, axis):
    n = lax.axis_size(axis)
    return exchange(jnp.broadcast_to(value[None], (n, *value.shape)), axis)


def summed(blocks):
    return jnp.sum(blocks.astype(F32), axis=0)


def pieces(value):
    high = lax.reduce_precision(value, 8, 7)
    rest = value - high
    middle = lax.reduce_precision(rest, 8, 7)
    return [p.astype(BF) for p in (high, middle, rest - middle)]


def columns(*values):
    return jnp.stack([p for v in values for p in pieces(v)], axis=-1)


def column(lanes, index):
    return jnp.sum(lanes[..., 3 * index : 3 * index + 3].astype(F32), axis=-1)


def swap(value, axis, bits):
    return lax.ppermute(value, axis, [(i, i ^ bits) for i in range(lax.axis_size(axis))])


def other_core(value):
    return swap(value, "co", 1)


def dot(a, b, contract):
    return lax.dot_general(a, b, ((contract[:1], contract[1:]), ((), ())), preferred_element_type=F32)


VMEM = pl.BlockSpec(memory_space=pltpu.VMEM)


def local_call(kernel, out, *args, scratch=(), scalar=False):
    specs = [VMEM] * len(args)
    if scalar:
        specs[0] = pl.BlockSpec(memory_space=pltpu.SMEM)
    return pl.pallas_call(
        kernel,
        out_shape=out,
        in_specs=specs,
        out_specs=jax.tree.map(lambda _: VMEM, out),
        scratch_shapes=scratch,
        compiler_params=pltpu.CompilerParams(vmem_limit_bytes=40 * 1024 * 1024),
    )(*args)


def fill_kernel(y_ref, both_ref, up_ref, down_ref, extra_ref, out_ref):
    n, block, _ = out_ref.shape
    local, hid = up_ref.shape
    part = jnp.dot(y_ref[...], up_ref[...], preferred_element_type=F32).astype(BF)
    out_ref[:, :, :hid] = part.reshape(n, block, hid)
    part = dot(both_ref[:, local:], down_ref[...], (1, 1)).astype(BF)
    out_ref[:, :, hid : 2 * hid] = part.reshape(n, block, hid)
    out_ref[:, :, 2 * hid :] = extra_ref[...]


def lane_pieces(values, lane):
    out = jnp.zeros(lane.shape, F32)
    for i, value in enumerate(values):
        for j in range(3):
            piece = value.astype(BF).astype(F32)
            out = jnp.where(lane == 3 * i + j, piece, out)
            value = value - piece
    return out


def halves(index, own_ref, peer_ref):
    tall = own_ref.shape[0]
    for ref, which in ((own_ref, index), (peer_ref, 1 - index)):
        yield ref, which, pl.ds(pl.multiple_of(which * tall, 16), tall)


def tokens_kernel(
    place_ref, own_ref, peer_ref, both_ref, up_ref, tilt_ref, gain_ref, tail_ref, z_ref
):
    n, high, _ = tail_ref.shape
    local, hid = up_ref.shape
    rows = both_ref.shape[0] // n
    rest = 0.0
    for ref, which, span in halves(place_ref[1], own_ref, peer_ref):
        grad = ref[:, hid : 2 * hid]
        marks = ref[:, 2 * hid :].astype(F32)
        lane = lax.broadcasted_iota(jnp.int32, marks.shape, 1)

        def taken(index):
            mine = (lane >= 3 * index) & (lane < 3 * index + 3)
            return jnp.sum(jnp.where(mine, marks, 0.0), axis=1, keepdims=True)

        cross, mean, inv = (taken(i) for i in range(3))
        normed = (both_ref[span, :local].astype(F32) - mean) * inv
        z_ref[span, :] = (normed * gain_ref[...]).astype(BF)
        d_z = dot(grad, up_ref[...], (1, 1))
        level = jnp.sum(grad.astype(F32) * tilt_ref[...], axis=1, keepdims=True)
        blocks = pl.ds(which * (n // 2), n // 2)
        tail_ref[blocks, :rows, :local] = d_z.astype(BF).reshape(n // 2, rows, local)
        sums = lane_pieces((level, cross), lane).astype(BF)
        tail_ref[blocks, :rows, local:] = sums.reshape(n // 2, rows, LANES)
        rest = rest + jnp.sum(d_z * normed, axis=0, keepdims=True)
    row = lax.broadcasted_iota(jnp.int32, (high - rows, local), 0)
    gains = jnp.zeros(row.shape, F32)
    for j in range(3):
        piece = rest.astype(BF).astype(F32)
        gains = jnp.where(row == j, piece, gains)
        rest = rest - piece
    gains = gains.astype(BF)
    for i in range(n):
        tail_ref[i, rows:, :local] = gains
        tail_ref[i, rows:, local:] = jnp.zeros((high - rows, LANES), BF)


def grads_kernel(
    place_ref, own_ref, peer_ref, both_ref, z_ref, keep_ref, give_ref, down_ref, up_ref
):
    hid, local = down_ref.shape
    down, up = 0.0, 0.0
    for ref, _, span in halves(place_ref[1], own_ref, peer_ref):
        down = down + dot(ref[:, :hid], both_ref[span, local:], (0, 0))
        up = up + dot(z_ref[span, :], ref[:, hid : 2 * hid], (0, 0))
    down_ref[...] = down.astype(BF)
    up_ref[...] = up.astype(BF)
    core = place_ref[0]
    n = keep_ref.shape[0]
    for ref, which in ((keep_ref, core), (give_ref, 1 - core)):
        for j in range(n):
            first = 0
            for whole in (down_ref, up_ref):
                height = whole.shape[0] // (2 * n)
                start = pl.multiple_of((2 * j + which) * height, 16)
                for i in range(0, whole.shape[1], LANES):
                    ref[j, first : first + height, :] = whole[pl.ds(start, height), i : i + LANES]
                    first += height


def merge_kernel(*refs):
    *parts, down_ref, up_ref = refs
    first = 0
    for out in (down_ref, up_ref):
        height = out.shape[0]
        for i in range(0, out.shape[1], LANES):
            total = sum(p[first : first + height, :].astype(F32) for p in parts)
            out[:, i : i + LANES] = total.astype(BF)
            first += height


def body(x_in, gain, w_up, w_down, d_out):
    rows, local = x_in.shape
    n_gx, n_yl, n_gz = (lax.axis_size(a) for a in ("gx", "yl", GZ))
    width = local * n_gz
    up_rows, hid = w_up.shape
    down_rows = w_down.shape[0]
    all_rows = rows * n_gx
    block = all_rows // n_gz
    even = lax.axis_index("co") == 0

    def by_core(mine, other):
        pair = [jnp.where(even, mine, other), jnp.where(even, other, mine)]
        return jnp.stack(pair, axis=1).reshape(-1, mine.shape[-1])

    down_full = lax.all_gather(w_down, GY, axis=0, tiled=True)
    up_mine = spread(w_up, "yl")
    both = lax.all_gather(jnp.concatenate([x_in, d_out], axis=1), "gx", axis=0, tiled=True)
    both, up_mine = lax.optimization_barrier((both, up_mine))
    up_full = by_core(up_mine, other_core(up_mine))
    x_rows = both[:, :local].astype(F32)

    part_sum = jnp.sum(x_rows, axis=1)
    off = x_rows - (part_sum / local)[:, None]
    second = jnp.sum(off * off, axis=1)
    y = (off * gain).astype(BF)
    gains = jnp.pad(jnp.stack(pieces(gain)), ((0, 5), (0, 0)))
    tilt = jnp.sum(dot(gains, up_full, (1, 0)), axis=0)
    tilt = jnp.stack(pieces(tilt)).reshape(3 * n_gz, -1)
    spare = LANES - tilt.shape[1]
    tilt = jnp.pad(tilt, ((0, block - tilt.shape[0]), (0, 0)))
    marks = columns(part_sum, second)
    extra = jnp.concatenate(
        [
            jnp.pad(marks, ((0, 0), (0, spare - marks.shape[1]))).reshape(n_gz, block, spare),
            jnp.broadcast_to(tilt, (n_gz, *tilt.shape)),
        ],
        axis=2,
    )
    pair = local_call(
        fill_kernel,
        jax.ShapeDtypeStruct((n_gz, block, 2 * hid + LANES), BF),
        *(y, both, up_full, down_full, extra),
    )
    pair = exchange(pair, GZ)
    marks = pair[:, :, 2 * hid : 2 * hid + spare]
    tilts = pair[:, : 3 * n_gz, 2 * hid + spare :].astype(F32)
    tilts = jnp.sum(tilts.reshape(n_gz, 3, n_gz, -1), axis=1).reshape(n_gz, hid)
    means = column(marks, 0) / local
    mean = jnp.sum(means, axis=0) / n_gz
    shift = means - mean
    var = (jnp.sum(column(marks, 1), axis=0) + local * jnp.sum(shift * shift, axis=0)) / width
    inv = lax.rsqrt(var + 1e-05)
    hidden = summed(pair[:, :, :hid]) + sum(
        shift[i][:, None] * tilts[i][None] for i in range(n_gz)
    )
    hidden = hidden * inv[:, None]
    d_act = summed(pair[:, :, hid : 2 * hid])
    act_f, slope = gelu_pair(hidden)
    d_hidden = (d_act * slope).astype(BF)
    cross = jnp.sum(d_hidden.astype(F32) * hidden, axis=1)
    marks = columns(cross, mean, inv)
    marks = jnp.pad(marks, ((0, 0), (0, LANES - marks.shape[1])))
    acts = jnp.concatenate([act_f.astype(BF), d_hidden, marks], axis=1)
    peer = swap(acts, "yh", 1)
    own = spread(acts, "xx")
    own, peer = lax.optimization_barrier((own, peer))
    own, peer = (v.reshape(all_rows // 2, -1) for v in (own, spread(peer, "xx")))

    place = jnp.stack([lax.axis_index("co"), lax.axis_index("yh")])
    tail, z = local_call(
        tokens_kernel,
        (
            jax.ShapeDtypeStruct((n_gx, rows + 8, local + LANES), BF),
            jax.ShapeDtypeStruct((all_rows, local), BF),
        ),
        *(place, own, peer, both, up_full, jnp.sum(tilts, axis=0)[None], gain[None]),
        scalar=True,
    )
    tail = exchange(tail, "gx")

    packed = down_rows * (local // LANES) + up_rows * (hid // LANES)
    keep, give = local_call(
        grads_kernel,
        (jax.ShapeDtypeStruct((n_yl, packed, LANES), BF),) * 2,
        *(place, own, peer, both, z),
        scratch=(pltpu.VMEM((hid, local), BF), pltpu.VMEM((local, hid), BF)),
        scalar=True,
    )
    grads = (keep.astype(F32) + other_core(give).astype(F32)).astype(BF)
    turn = lax.axis_index("yl")

    def part(index):
        return lax.dynamic_index_in_dim(grads, index, keepdims=False)

    grads = [part(turn)] + [swap(part(turn ^ k), "yl", k) for k in range(1, n_yl)]
    d_z = summed(tail[:, :rows, :local])
    marks = summed(tail[:, :rows, local:])
    scaled_sum, cross_sum = (column(marks, i)[:, None] / width for i in range(2))
    d_gain = jnp.sum(tail[:, rows : rows + 3, :local].astype(F32), axis=(0, 1))
    for axis, bits in (("yl", 1), ("yl", 2), ("co", 1)):
        d_gain = d_gain + swap(d_gain, axis, bits)

    d_w_down, d_w_up = local_call(
        merge_kernel,
        (
            jax.ShapeDtypeStruct((down_rows, local), BF),
            jax.ShapeDtypeStruct((up_rows, hid), BF),
        ),
        *grads,
    )

    first = lax.axis_index("gx") * rows

    half = n_gx // 2
    marks = jnp.where(lax.axis_index("yh") == first // (rows * half), own, peer)
    marks = marks.reshape(half, rows, -1)[:, :, 2 * hid :]
    marks = lax.dynamic_index_in_dim(marks, lax.axis_index("gx") % half, keepdims=False)
    own_mean, own_inv = column(marks, 1)[:, None], column(marks, 2)[:, None]
    own_normed = (x_in.astype(F32) - own_mean) * own_inv
    d_x = own_inv * (d_z * gain - scaled_sum - own_normed * cross_sum)
    return (d_x.astype(BF), d_w_up, d_w_down, d_gain)


def solution(mesh):
    sizes = mesh.shape
    cores, x_chips = 2, sizes["gz"] // 2
    fine = Mesh(
        mesh.devices.reshape(sizes["gx"], sizes["gy"] // cores, cores, 2, x_chips),
        ("gx", *GY, *GZ),
    )
    placed = (
        P((*GY, "gx"), GZ),
        P(GZ),
        P((*GZ, *GY), "gx"),
        P(("gx", *GY), GZ),
        P((*GY, "gx"), GZ),
    )
    return jax.shard_map(
        body,
        mesh=fine,
        in_specs=placed,
        out_specs=(P((*GY, "gx"), GZ), P((*GZ, *GY), "gx"), P(("gx", *GY), GZ), P(GZ)),
        check_vma=False,
    )
```

```python
import jax
import jax.numpy as jnp
from jax import lax
from jax.experimental import pallas as pl
from jax.experimental.pallas import tpu as pltpu
from jax.sharding import Mesh
from jax.sharding import PartitionSpec as P

BF, F32 = jnp.bfloat16, jnp.float32
LANES = 128
GY, GZ = ("yl", "co"), ("yh", "xx")


def gelu_pair(hidden):
    cdf = 0.5 * (1.0 + jax.scipy.special.erf(hidden * 0.7071067811865476))
    slope = cdf + hidden * jnp.exp(-0.5 * hidden * hidden) * 0.3989422804014327
    return (hidden * cdf, slope)


def exchange(blocks, axis):
    return lax.all_to_all(blocks, axis, 0, 0, tiled=True)


def spread(value, axis):
    n = lax.axis_size(axis)
    return exchange(jnp.broadcast_to(value[None], (n, *value.shape)), axis)


def summed(blocks):
    return jnp.sum(blocks.astype(F32), axis=0)


def pieces(value):
    high = lax.reduce_precision(value, 8, 7)
    rest = value - high
    middle = lax.reduce_precision(rest, 8, 7)
    return [p.astype(BF) for p in (high, middle, rest - middle)]


def columns(*values):
    return jnp.stack([p for v in values for p in pieces(v)], axis=-1)


def column(lanes, index):
    return jnp.sum(lanes[..., 3 * index : 3 * index + 3].astype(F32), axis=-1)


def swap(value, axis, bits):
    return lax.ppermute(value, axis, [(i, i ^ bits) for i in range(lax.axis_size(axis))])


def other_core(value):
    return swap(value, "co", 1)


def dot(a, b, contract):
    return lax.dot_general(a, b, ((contract[:1], contract[1:]), ((), ())), preferred_element_type=F32)


VMEM = pl.BlockSpec(memory_space=pltpu.VMEM)


def local_call(kernel, out, *args, scratch=(), scalar=False):
    specs = [VMEM] * len(args)
    if scalar:
        specs[0] = pl.BlockSpec(memory_space=pltpu.SMEM)
    return pl.pallas_call(
        kernel,
        out_shape=out,
        in_specs=specs,
        out_specs=jax.tree.map(lambda _: VMEM, out),
        scratch_shapes=scratch,
        compiler_params=pltpu.CompilerParams(vmem_limit_bytes=40 * 1024 * 1024),
    )(*args)


def fill_kernel(y_ref, both_ref, up_ref, down_ref, extra_ref, out_ref):
    n, block, _ = out_ref.shape
    local, hid = up_ref.shape
    part = jnp.dot(y_ref[...], up_ref[...], preferred_element_type=F32).astype(BF)
    out_ref[:, :, :hid] = part.reshape(n, block, hid)
    part = dot(both_ref[:, local:], down_ref[...], (1, 1)).astype(BF)
    out_ref[:, :, hid : 2 * hid] = part.reshape(n, block, hid)
    out_ref[:, :, 2 * hid :] = extra_ref[...]


def lane_pieces(values, lane):
    out = jnp.zeros(lane.shape, F32)
    for i, value in enumerate(values):
        for j in range(3):
            piece = value.astype(BF).astype(F32)
            out = jnp.where(lane == 3 * i + j, piece, out)
            value = value - piece
    return out


def halves(index, own_ref, peer_ref):
    tall = own_ref.shape[0]
    for ref, which in ((own_ref, index), (peer_ref, 1 - index)):
        yield ref, which, pl.ds(pl.multiple_of(which * tall, 16), tall)


def tokens_kernel(
    place_ref, own_ref, peer_ref, both_ref, up_ref, tilt_ref, gain_ref, tail_ref, z_ref
):
    n, high, _ = tail_ref.shape
    local, hid = up_ref.shape
    rows = both_ref.shape[0] // n
    rest = 0.0
    for ref, which, span in halves(place_ref[1], own_ref, peer_ref):
        grad = ref[:, hid : 2 * hid]
        marks = ref[:, 2 * hid :].astype(F32)
        lane = lax.broadcasted_iota(jnp.int32, marks.shape, 1)

        def taken(index):
            mine = (lane >= 3 * index) & (lane < 3 * index + 3)
            return jnp.sum(jnp.where(mine, marks, 0.0), axis=1, keepdims=True)

        cross, mean, inv = (taken(i) for i in range(3))
        normed = (both_ref[span, :local].astype(F32) - mean) * inv
        z_ref[span, :] = (normed * gain_ref[...]).astype(BF)
        d_z = dot(grad, up_ref[...], (1, 1))
        level = jnp.sum(grad.astype(F32) * tilt_ref[...], axis=1, keepdims=True)
        blocks = pl.ds(which * (n // 2), n // 2)
        tail_ref[blocks, :rows, :local] = d_z.astype(BF).reshape(n // 2, rows, local)
        sums = lane_pieces((level, cross), lane).astype(BF)
        tail_ref[blocks, :rows, local:] = sums.reshape(n // 2, rows, LANES)
        rest = rest + jnp.sum(d_z * normed, axis=0, keepdims=True)
    row = lax.broadcasted_iota(jnp.int32, (high - rows, local), 0)
    gains = jnp.zeros(row.shape, F32)
    for j in range(3):
        piece = rest.astype(BF).astype(F32)
        gains = jnp.where(row == j, piece, gains)
        rest = rest - piece
    gains = gains.astype(BF)
    for i in range(n):
        tail_ref[i, rows:, :local] = gains
        tail_ref[i, rows:, local:] = jnp.zeros((high - rows, LANES), BF)


def grads_kernel(
    place_ref, own_ref, peer_ref, both_ref, z_ref, keep_ref, give_ref, down_ref, up_ref, all_ref
):
    hid, local = down_ref.shape
    for ref, _, span in halves(place_ref[1], own_ref, peer_ref):
        all_ref[span, :] = ref[:, : 2 * hid]
    down_ref[...] = dot(all_ref[:, :hid], both_ref[:, local:], (0, 0)).astype(BF)
    up_ref[...] = dot(z_ref[...], all_ref[:, hid:], (0, 0)).astype(BF)
    core = place_ref[0]
    n = keep_ref.shape[0]
    for ref, which in ((keep_ref, core), (give_ref, 1 - core)):
        for j in range(n):
            first = 0
            for whole in (down_ref, up_ref):
                height = whole.shape[0] // (2 * n)
                start = pl.multiple_of((2 * j + which) * height, 16)
                for i in range(0, whole.shape[1], LANES):
                    ref[j, first : first + height, :] = whole[pl.ds(start, height), i : i + LANES]
                    first += height


def merge_kernel(*refs):
    *parts, down_ref, up_ref = refs
    first = 0
    for out in (down_ref, up_ref):
        height = out.shape[0]
        for i in range(0, out.shape[1], LANES):
            total = sum(p[first : first + height, :].astype(F32) for p in parts)
            out[:, i : i + LANES] = total.astype(BF)
            first += height


def body(x_in, gain, w_up, w_down, d_out):
    rows, local = x_in.shape
    n_gx, n_yl, n_gz = (lax.axis_size(a) for a in ("gx", "yl", GZ))
    width = local * n_gz
    up_rows, hid = w_up.shape
    down_rows = w_down.shape[0]
    all_rows = rows * n_gx
    block = all_rows // n_gz
    even = lax.axis_index("co") == 0

    def by_core(mine, other):
        pair = [jnp.where(even, mine, other), jnp.where(even, other, mine)]
        return jnp.stack(pair, axis=1).reshape(-1, mine.shape[-1])

    down_full = lax.all_gather(w_down, GY, axis=0, tiled=True)
    up_mine = spread(w_up, "yl")
    both = lax.all_gather(jnp.concatenate([x_in, d_out], axis=1), "gx", axis=0, tiled=True)
    both, up_mine = lax.optimization_barrier((both, up_mine))
    up_full = by_core(up_mine, other_core(up_mine))
    x_rows = both[:, :local].astype(F32)

    part_sum = jnp.sum(x_rows, axis=1)
    off = x_rows - (part_sum / local)[:, None]
    second = jnp.sum(off * off, axis=1)
    y = (off * gain).astype(BF)
    gains = jnp.pad(jnp.stack(pieces(gain)), ((0, 5), (0, 0)))
    tilt = jnp.sum(dot(gains, up_full, (1, 0)), axis=0)
    tilt = jnp.stack(pieces(tilt)).reshape(3 * n_gz, -1)
    spare = LANES - tilt.shape[1]
    tilt = jnp.pad(tilt, ((0, block - tilt.shape[0]), (0, 0)))
    marks = columns(part_sum, second)
    extra = jnp.concatenate(
        [
            jnp.pad(marks, ((0, 0), (0, spare - marks.shape[1]))).reshape(n_gz, block, spare),
            jnp.broadcast_to(tilt, (n_gz, *tilt.shape)),
        ],
        axis=2,
    )
    pair = local_call(
        fill_kernel,
        jax.ShapeDtypeStruct((n_gz, block, 2 * hid + LANES), BF),
        *(y, both, up_full, down_full, extra),
    )
    pair = exchange(pair, GZ)
    marks = pair[:, :, 2 * hid : 2 * hid + spare]
    tilts = pair[:, : 3 * n_gz, 2 * hid + spare :].astype(F32)
    tilts = jnp.sum(tilts.reshape(n_gz, 3, n_gz, -1), axis=1).reshape(n_gz, hid)
    means = column(marks, 0) / local
    mean = jnp.sum(means, axis=0) / n_gz
    shift = means - mean
    var = (jnp.sum(column(marks, 1), axis=0) + local * jnp.sum(shift * shift, axis=0)) / width
    inv = lax.rsqrt(var + 1e-05)
    hidden = summed(pair[:, :, :hid]) + sum(
        shift[i][:, None] * tilts[i][None] for i in range(n_gz)
    )
    hidden = hidden * inv[:, None]
    d_act = summed(pair[:, :, hid : 2 * hid])
    act_f, slope = gelu_pair(hidden)
    d_hidden = (d_act * slope).astype(BF)
    cross = jnp.sum(d_hidden.astype(F32) * hidden, axis=1)
    marks = columns(cross, mean, inv)
    marks = jnp.pad(marks, ((0, 0), (0, LANES - marks.shape[1])))
    acts = jnp.concatenate([act_f.astype(BF), d_hidden, marks], axis=1)
    peer = swap(acts, "yh", 1)
    own = spread(acts, "xx")
    own, peer = lax.optimization_barrier((own, peer))
    own, peer = (v.reshape(all_rows // 2, -1) for v in (own, spread(peer, "xx")))

    place = jnp.stack([lax.axis_index("co"), lax.axis_index("yh")])
    tail, z = local_call(
        tokens_kernel,
        (
            jax.ShapeDtypeStruct((n_gx, rows + 8, local + LANES), BF),
            jax.ShapeDtypeStruct((all_rows, local), BF),
        ),
        *(place, own, peer, both, up_full, jnp.sum(tilts, axis=0)[None], gain[None]),
        scalar=True,
    )
    tail = exchange(tail, "gx")

    packed = down_rows * (local // LANES) + up_rows * (hid // LANES)
    keep, give = local_call(
        grads_kernel,
        (jax.ShapeDtypeStruct((n_yl, packed, LANES), BF),) * 2,
        *(place, own, peer, both, z),
        scratch=[pltpu.VMEM(v, BF) for v in ((hid, local), (local, hid), (all_rows, 2 * hid))],
        scalar=True,
    )
    grads = (keep.astype(F32) + other_core(give).astype(F32)).astype(BF)
    turn = lax.axis_index("yl")

    def part(index):
        return lax.dynamic_index_in_dim(grads, index, keepdims=False)

    grads = [part(turn)] + [swap(part(turn ^ k), "yl", k) for k in range(1, n_yl)]
    d_z = summed(tail[:, :rows, :local])
    marks = summed(tail[:, :rows, local:])
    scaled_sum, cross_sum = (column(marks, i)[:, None] / width for i in range(2))
    d_gain = jnp.sum(tail[:, rows : rows + 3, :local].astype(F32), axis=(0, 1))
    for axis, bits in (("yl", 1), ("yl", 2), ("co", 1)):
        d_gain = d_gain + swap(d_gain, axis, bits)

    d_w_down, d_w_up = local_call(
        merge_kernel,
        (
            jax.ShapeDtypeStruct((down_rows, local), BF),
            jax.ShapeDtypeStruct((up_rows, hid), BF),
        ),
        *grads,
    )

    first = lax.axis_index("gx") * rows

    half = n_gx // 2
    own, peer, d_z = lax.optimization_barrier((own, peer, d_z))
    marks = jnp.where(lax.axis_index("yh") == first // (rows * half), own, peer)
    marks = marks.reshape(half, rows, -1)[:, :, 2 * hid :]
    marks = lax.dynamic_index_in_dim(marks, lax.axis_index("gx") % half, keepdims=False)
    own_mean, own_inv = column(marks, 1)[:, None], column(marks, 2)[:, None]
    own_normed = (x_in.astype(F32) - own_mean) * own_inv
    d_x = own_inv * (d_z * gain - scaled_sum - own_normed * cross_sum)
    return (d_x.astype(BF), d_w_up, d_w_down, d_gain)


def solution(mesh):
    sizes = mesh.shape
    cores, x_chips = 2, sizes["gz"] // 2
    fine = Mesh(
        mesh.devices.reshape(sizes["gx"], sizes["gy"] // cores, cores, 2, x_chips),
        ("gx", *GY, *GZ),
    )
    placed = (
        P((*GY, "gx"), GZ),
        P(GZ),
        P((*GZ, *GY), "gx"),
        P(("gx", *GY), GZ),
        P((*GY, "gx"), GZ),
    )
    return jax.shard_map(
        body,
        mesh=fine,
        in_specs=placed,
        out_specs=(P((*GY, "gx"), GZ), P((*GZ, *GY), "gx"), P(("gx", *GY), GZ), P(GZ)),
        check_vma=False,
    )
```

```python
import jax
import jax.numpy as jnp
from jax import lax
from jax.experimental import pallas as pl
from jax.experimental.pallas import tpu as pltpu
from jax.sharding import Mesh
from jax.sharding import PartitionSpec as P

BF, F32 = jnp.bfloat16, jnp.float32
LANES = 128
GY, GZ = ("yl", "co"), ("yh", "xx")


def gelu_pair(hidden):
    cdf = 0.5 * (1.0 + jax.scipy.special.erf(hidden * 0.7071067811865476))
    slope = cdf + hidden * jnp.exp(-0.5 * hidden * hidden) * 0.3989422804014327
    return (hidden * cdf, slope)


def exchange(blocks, axis):
    return lax.all_to_all(blocks, axis, 0, 0, tiled=True)


def spread(value, axis):
    n = lax.axis_size(axis)
    return exchange(jnp.broadcast_to(value[None], (n, *value.shape)), axis)


def summed(blocks):
    return jnp.sum(blocks.astype(F32), axis=0)


def pieces(value):
    high = lax.reduce_precision(value, 8, 7)
    rest = value - high
    middle = lax.reduce_precision(rest, 8, 7)
    return [p.astype(BF) for p in (high, middle, rest - middle)]


def columns(*values):
    return jnp.stack([p for v in values for p in pieces(v)], axis=-1)


def column(lanes, index):
    return jnp.sum(lanes[..., 3 * index : 3 * index + 3].astype(F32), axis=-1)


def swap(value, axis, bits):
    return lax.ppermute(value, axis, [(i, i ^ bits) for i in range(lax.axis_size(axis))])


def other_core(value):
    return swap(value, "co", 1)


def dot(a, b, contract):
    return lax.dot_general(a, b, ((contract[:1], contract[1:]), ((), ())), preferred_element_type=F32)


VMEM = pl.BlockSpec(memory_space=pltpu.VMEM)


def local_call(kernel, out, *args, scratch=(), scalar=False):
    specs = [VMEM] * len(args)
    if scalar:
        specs[0] = pl.BlockSpec(memory_space=pltpu.SMEM)
    return pl.pallas_call(
        kernel,
        out_shape=out,
        in_specs=specs,
        out_specs=jax.tree.map(lambda _: VMEM, out),
        scratch_shapes=scratch,
        compiler_params=pltpu.CompilerParams(vmem_limit_bytes=40 * 1024 * 1024),
    )(*args)


def fill_kernel(y_ref, both_ref, up_ref, down_ref, extra_ref, out_ref):
    n, block, _ = out_ref.shape
    local, hid = up_ref.shape
    part = jnp.dot(y_ref[...], up_ref[...], preferred_element_type=F32).astype(BF)
    out_ref[:, :, :hid] = part.reshape(n, block, hid)
    part = dot(both_ref[:, local:], down_ref[...], (1, 1)).astype(BF)
    out_ref[:, :, hid : 2 * hid] = part.reshape(n, block, hid)
    out_ref[:, :, 2 * hid :] = extra_ref[...]


def lane_pieces(values, lane):
    out = jnp.zeros(lane.shape, F32)
    for i, value in enumerate(values):
        for j in range(3):
            piece = value.astype(BF).astype(F32)
            out = jnp.where(lane == 3 * i + j, piece, out)
            value = value - piece
    return out


def halves(index, own_ref, peer_ref):
    tall = own_ref.shape[0]
    for ref, which in ((own_ref, index), (peer_ref, 1 - index)):
        yield ref, which, pl.ds(pl.multiple_of(which * tall, 16), tall)


def tokens_kernel(
    place_ref, own_ref, peer_ref, both_ref, up_ref, tilt_ref, gain_ref, tail_ref, z_ref
):
    n, high, _ = tail_ref.shape
    local, hid = up_ref.shape
    rows = both_ref.shape[0] // n
    rest = 0.0
    for ref, which, span in halves(place_ref[1], own_ref, peer_ref):
        grad = ref[:, hid : 2 * hid]
        marks = ref[:, 2 * hid :].astype(F32)
        lane = lax.broadcasted_iota(jnp.int32, marks.shape, 1)

        def taken(index):
            mine = (lane >= 3 * index) & (lane < 3 * index + 3)
            return jnp.sum(jnp.where(mine, marks, 0.0), axis=1, keepdims=True)

        cross, mean, inv = (taken(i) for i in range(3))
        normed = (both_ref[span, :local].astype(F32) - mean) * inv
        z_ref[span, :] = (normed * gain_ref[...]).astype(BF)
        d_z = dot(grad, up_ref[...], (1, 1))
        level = jnp.sum(grad.astype(F32) * tilt_ref[...], axis=1, keepdims=True)
        blocks = pl.ds(which * (n // 2), n // 2)
        tail_ref[blocks, :rows, :local] = d_z.astype(BF).reshape(n // 2, rows, local)
        sums = lane_pieces((level, cross), lane).astype(BF)
        tail_ref[blocks, :rows, local:] = sums.reshape(n // 2, rows, LANES)
        rest = rest + jnp.sum(d_z * normed, axis=0, keepdims=True)
    row = lax.broadcasted_iota(jnp.int32, (high - rows, local), 0)
    gains = jnp.zeros(row.shape, F32)
    for j in range(3):
        piece = rest.astype(BF).astype(F32)
        gains = jnp.where(row == j, piece, gains)
        rest = rest - piece
    gains = gains.astype(BF)
    for i in range(n):
        tail_ref[i, rows:, :local] = gains
        tail_ref[i, rows:, local:] = jnp.zeros((high - rows, LANES), BF)


def grads_kernel(
    place_ref, own_ref, peer_ref, both_ref, z_ref, keep_ref, give_ref, down_ref, up_ref, all_ref
):
    hid, local = down_ref.shape
    for ref, _, span in halves(place_ref[1], own_ref, peer_ref):
        all_ref[span, :] = ref[:, : 2 * hid]
    down_ref[...] = dot(all_ref[:, :hid], both_ref[:, local:], (0, 0)).astype(BF)
    up_ref[...] = dot(z_ref[...], all_ref[:, hid:], (0, 0)).astype(BF)
    core = place_ref[0]
    n = keep_ref.shape[0]
    for ref, which in ((keep_ref, core), (give_ref, 1 - core)):
        for j in range(n):
            first = 0
            for whole in (down_ref, up_ref):
                height = whole.shape[0] // (2 * n)
                start = pl.multiple_of((2 * j + which) * height, 16)
                for i in range(0, whole.shape[1], LANES):
                    ref[j, first : first + height, :] = whole[pl.ds(start, height), i : i + LANES]
                    first += height


def merge_kernel(*refs):
    *parts, down_ref, up_ref = refs
    first = 0
    for out in (down_ref, up_ref):
        height = out.shape[0]
        for i in range(0, out.shape[1], LANES):
            total = sum(p[first : first + height, :].astype(F32) for p in parts)
            out[:, i : i + LANES] = total.astype(BF)
            first += height


def body(x_in, gain, w_up, w_down, d_out):
    rows, local = x_in.shape
    n_gx, n_yl, n_gz = (lax.axis_size(a) for a in ("gx", "yl", GZ))
    width = local * n_gz
    up_rows, hid = w_up.shape
    down_rows = w_down.shape[0]
    all_rows = rows * n_gx
    block = all_rows // n_gz
    even = lax.axis_index("co") == 0

    def by_core(mine, other):
        pair = [jnp.where(even, mine, other), jnp.where(even, other, mine)]
        return jnp.stack(pair, axis=1).reshape(-1, mine.shape[-1])

    down_full = lax.all_gather(w_down, GY, axis=0, tiled=True)
    up_mine = spread(w_up, "yl")
    both = lax.all_gather(jnp.concatenate([x_in, d_out], axis=1), "gx", axis=0, tiled=True)
    both, up_mine = lax.optimization_barrier((both, up_mine))
    up_full = by_core(up_mine, other_core(up_mine))
    x_rows = both[:, :local].astype(F32)

    part_sum = jnp.sum(x_rows, axis=1)
    off = x_rows - (part_sum / local)[:, None]
    second = jnp.sum(off * off, axis=1)
    y = (off * gain).astype(BF)
    gains = jnp.pad(jnp.stack(pieces(gain)), ((0, 5), (0, 0)))
    tilt = jnp.sum(dot(gains, up_full, (1, 0)), axis=0)
    tilt = jnp.stack(pieces(tilt)).reshape(3 * n_gz, -1)
    spare = LANES - tilt.shape[1]
    tilt = jnp.pad(tilt, ((0, block - tilt.shape[0]), (0, 0)))
    marks = columns(part_sum, second)
    extra = jnp.concatenate(
        [
            jnp.pad(marks, ((0, 0), (0, spare - marks.shape[1]))).reshape(n_gz, block, spare),
            jnp.broadcast_to(tilt, (n_gz, *tilt.shape)),
        ],
        axis=2,
    )
    pair = local_call(
        fill_kernel,
        jax.ShapeDtypeStruct((n_gz, block, 2 * hid + LANES), BF),
        *(y, both, up_full, down_full, extra),
    )
    pair = exchange(pair, GZ)
    marks = pair[:, :, 2 * hid : 2 * hid + spare]
    tilts = pair[:, : 3 * n_gz, 2 * hid + spare :].astype(F32)
    tilts = jnp.sum(tilts.reshape(n_gz, 3, n_gz, -1), axis=1).reshape(n_gz, hid)
    means = column(marks, 0) / local
    mean = jnp.sum(means, axis=0) / n_gz
    shift = means - mean
    var = (jnp.sum(column(marks, 1), axis=0) + local * jnp.sum(shift * shift, axis=0)) / width
    inv = lax.rsqrt(var + 1e-05)
    hidden = summed(pair[:, :, :hid]) + sum(
        shift[i][:, None] * tilts[i][None] for i in range(n_gz)
    )
    hidden = hidden * inv[:, None]
    d_act = summed(pair[:, :, hid : 2 * hid])
    act_f, slope = gelu_pair(hidden)
    d_hidden = (d_act * slope).astype(BF)
    cross = jnp.sum(d_hidden.astype(F32) * hidden, axis=1)
    marks = columns(cross, mean, inv)
    marks = jnp.pad(marks, ((0, 0), (0, LANES - marks.shape[1])))
    acts = jnp.concatenate([act_f.astype(BF), d_hidden, marks], axis=1)
    peer = swap(acts, "yh", 1)
    got1 = swap(acts, "xx", 1)
    got2 = swap(acts, "xx", 2)
    got3 = swap(acts, "xx", 3)
    spot = lax.axis_index("xx")
    got = jnp.stack([acts, got1, got2, got3])
    own = jnp.concatenate(
        [lax.dynamic_index_in_dim(got, spot ^ i, keepdims=False) for i in range(got.shape[0])]
    )
    peer = spread(peer, "xx").reshape(all_rows // 2, -1)

    place = jnp.stack([lax.axis_index("co"), lax.axis_index("yh")])
    tail, z = local_call(
        tokens_kernel,
        (
            jax.ShapeDtypeStruct((n_gx, rows + 8, local + LANES), BF),
            jax.ShapeDtypeStruct((all_rows, local), BF),
        ),
        *(place, own, peer, both, up_full, jnp.sum(tilts, axis=0)[None], gain[None]),
        scalar=True,
    )
    tail = exchange(tail, "gx")

    packed = down_rows * (local // LANES) + up_rows * (hid // LANES)
    keep, give = local_call(
        grads_kernel,
        (jax.ShapeDtypeStruct((n_yl, packed, LANES), BF),) * 2,
        *(place, own, peer, both, z),
        scratch=[pltpu.VMEM(v, BF) for v in ((hid, local), (local, hid), (all_rows, 2 * hid))],
        scalar=True,
    )
    grads = (keep.astype(F32) + other_core(give).astype(F32)).astype(BF)
    turn = lax.axis_index("yl")

    def part(index):
        return lax.dynamic_index_in_dim(grads, index, keepdims=False)

    grads = [part(turn)] + [swap(part(turn ^ k), "yl", k) for k in range(1, n_yl)]
    d_z = summed(tail[:, :rows, :local])
    marks = summed(tail[:, :rows, local:])
    scaled_sum, cross_sum = (column(marks, i)[:, None] / width for i in range(2))
    d_gain = jnp.sum(tail[:, rows : rows + 3, :local].astype(F32), axis=(0, 1))
    for axis, bits in (("yl", 1), ("yl", 2), ("co", 1)):
        d_gain = d_gain + swap(d_gain, axis, bits)

    d_w_down, d_w_up = local_call(
        merge_kernel,
        (
            jax.ShapeDtypeStruct((down_rows, local), BF),
            jax.ShapeDtypeStruct((up_rows, hid), BF),
        ),
        *grads,
    )

    first = lax.axis_index("gx") * rows

    half = n_gx // 2
    own, peer, d_z = lax.optimization_barrier((own, peer, d_z))
    marks = jnp.where(lax.axis_index("yh") == first // (rows * half), own, peer)
    marks = marks.reshape(half, rows, -1)[:, :, 2 * hid :]
    marks = lax.dynamic_index_in_dim(marks, lax.axis_index("gx") % half, keepdims=False)
    own_mean, own_inv = column(marks, 1)[:, None], column(marks, 2)[:, None]
    own_normed = (x_in.astype(F32) - own_mean) * own_inv
    d_x = own_inv * (d_z * gain - scaled_sum - own_normed * cross_sum)
    return (d_x.astype(BF), d_w_up, d_w_down, d_gain)


def solution(mesh):
    sizes = mesh.shape
    cores, x_chips = 2, sizes["gz"] // 2
    fine = Mesh(
        mesh.devices.reshape(sizes["gx"], sizes["gy"] // cores, cores, 2, x_chips),
        ("gx", *GY, *GZ),
    )
    placed = (
        P((*GY, "gx"), GZ),
        P(GZ),
        P((*GZ, *GY), "gx"),
        P(("gx", *GY), GZ),
        P((*GY, "gx"), GZ),
    )
    return jax.shard_map(
        body,
        mesh=fine,
        in_specs=placed,
        out_specs=(P((*GY, "gx"), GZ), P((*GZ, *GY), "gx"), P(("gx", *GY), GZ), P(GZ)),
        check_vma=False,
    )
```
